32 devices in a mesh: shard: 4 (over z), tensor: 2 (over core), section: 4 (over y, x).
Axes of the slice: x: 2, y: 2, z: 4, core: 2. Of those that a mesh axis runs over, the one named last changes fastest.
Arguments:
- gradient: bfloat16 [2560, 2560], P('shard', ('tensor', 'section')), may hold values from -100 to 100
- gain_grad: float32 [2, 2560], P(None, 'shard'), may hold values from -12 to 12
- left_statistic: float32 [2560, 2560], P('shard', ('tensor', 'section')), may hold values from -1 to 3, as said below
- left_basis: float32 [2560, 2560], P('shard', ('tensor', 'section')), may hold values from -1 to 1.5
- first_moment: float32 [2560, 2560], P('shard', ('tensor', 'section')), may hold values from -3 to 3
- second_moment: float32 [2560, 2560], P('shard', ('tensor', 'section')), may hold values from 0.2 to 2
- norm_gains: float32 [2, 2560], P(None, 'shard'), may hold values from 0.5 to 1.5
- gain_first: float32 [2, 2560], P(None, 'shard'), may hold values from -2 to 2
- gain_second: float32 [2, 2560], P(None, 'shard'), may hold values from 0.5 to 5
Outputs:
- update: float32 [2560, 2560], P('shard', ('tensor', 'section'))
- new_first: float32 [2560, 2560], P('shard', ('tensor', 'section'))
- new_second: float32 [2560, 2560], P('shard', ('tensor', 'section'))
- new_statistic: float32 [2560, 2560], P('shard', ('tensor', 'section'))
- new_basis: float32 [2560, 2560], P('shard', ('tensor', 'section'))
- new_gains: float32 [2, 2560], P(None, 'shard')
- new_gain_first: float32 [2, 2560], P(None, 'shard')
- new_gain_second: float32 [2, 2560], P(None, 'shard')
The draws below stay inside these ranges and needn't reach their ends.
Inputs may be any that keep to these rules, and one draw needn't show every extreme that they name: `left_statistic`: symmetric.
All inputs are finite; a program needn't handle non-finite values.
Results may differ from the reference program's by a relative error of at most 0.0003.
Values may be sent and summed in bfloat16 or wider, within the bound.
A program may use at most 128 MiB of HBM per device.

```python
import math
import jax
import jax.numpy as jnp
from jax import lax

D = 2560
NS_STEPS = 3


def draw_gradient(key, part):
    base_key, row_key, col_key = jax.random.split(key, 3)
    positions = jnp.arange(D, dtype=jnp.float32)
    rising = jnp.exp(jnp.log(3.0) * positions / (D - 1))
    row_scale = rising * jnp.exp(jax.random.uniform(row_key, (D,), jnp.float32, 0.0, jnp.log(2.0)))
    col_scale = jnp.exp(jax.random.uniform(col_key, (D,), jnp.float32, 0.0, jnp.log(3.3)))
    base_values = jnp.clip(jax.random.normal(base_key, (D, D), jnp.float32), -5.0, 5.0)
    return (base_values * row_scale[:, None] * col_scale[None, :]).astype(jnp.bfloat16)


def draw_left_statistic(key, part):
    diag_key, noise_key = jax.random.split(jax.random.fold_in(key, 11), 2)
    diagonal = jnp.exp(jax.random.uniform(diag_key, (D,), jnp.float32, jnp.log(1.5), jnp.log(2.8)))
    noise = jax.random.uniform(noise_key, (D, D), jnp.float32, -1.0, 1.0)
    symmetric = (noise + noise.T) * (0.5 / jnp.sqrt(jnp.float32(D)))
    return symmetric + jnp.diag(diagonal)


def draw_left_basis(key, part):
    noise_key = jax.random.fold_in(key, 23)
    noise = jnp.clip(jax.random.normal(noise_key, (D, D), jnp.float32), -4.0, 4.0) * (0.2 / jnp.sqrt(jnp.float32(D)))
    return jnp.eye(D, dtype=jnp.float32) + noise


def shard_levels(rng, dims, pieces, least, largest):
    gain, own = 1.0, jax.random.fold_in(rng, 6)
    for position, shards_of in pieces:
        heights = jnp.exp(jax.random.uniform(jax.random.fold_in(own, position), (shards_of,), jnp.float32, least / len(pieces), largest / len(pieces)))
        gain = gain * jnp.repeat(heights, dims[position] // shards_of).reshape([-1 if axis == position else 1 for axis in range(len(dims))])
    return gain


def gaussian(stream_key, extent, spread, most, cuts=(), kind=jnp.bfloat16):
    factor_of = shard_levels(stream_key, extent, cuts, -0.22, 0.18) if cuts else 1.0
    result = jax.random.normal(stream_key, extent, jnp.float32) * spread * factor_of
    return jnp.minimum(jnp.maximum(result, -most), most).astype(kind)


def setup_inputs(seed: int = 0) -> dict:
    key_of = jax.random.split(jax.random.key(seed), 10)
    return {
        "gradient": draw_gradient(jax.random.fold_in(key_of[9], 71), 0),
        "gain_grad": gaussian(key_of[1], (2, D), 3.0, 12.0, ((1, 4),), jnp.float32),
        "left_statistic": draw_left_statistic(jax.random.fold_in(key_of[9], 71), 0),
        "left_basis": draw_left_basis(jax.random.fold_in(key_of[9], 71), 0),
        "first_moment": gaussian(key_of[4], (D, D), 0.5, 3.0, ((0, 4), (1, 8)), jnp.float32),
        "second_moment": jnp.clip(jnp.exp(math.log(2.0) - 2.3025851 * jax.random.uniform(key_of[5], (D, D), jnp.float32) ** shard_levels(key_of[5], (D, D), ((0, 4), (1, 8)), -0.2, 0.2)), 0.2, 2.0),
        "norm_gains": jnp.clip(1.0 + 0.1 * jax.random.normal(key_of[6], (2, D), jnp.float32), 0.5, 1.5),
        "gain_first": gaussian(key_of[7], (2, D), 0.3, 2.0, ((1, 4),), jnp.float32),
        "gain_second": jnp.clip(jnp.exp(math.log(5.0) - 2.3025851 * jax.random.uniform(key_of[8], (2, D), jnp.float32) ** shard_levels(key_of[8], (2, D), ((1, 4),), -0.2, 0.2)), 0.5, 5.0),
    }


def matmul(left_side, right_side):
    return jnp.dot(left_side, right_side, precision=lax.Precision.HIGHEST, preferred_element_type=jnp.float32)

def reference(gradient, gain_grad, left_statistic, left_basis, first_moment, second_moment, norm_gains, gain_first, gain_second):
    grad_float = gradient.astype(jnp.float32)
    squares_total = jnp.sum(grad_float * grad_float) + jnp.sum(gain_grad * gain_grad)
    clip_factor = jnp.minimum(1.0, D / jnp.sqrt(squares_total + 1e-06))
    clipped = clip_factor * grad_float
    rotated = matmul(left_basis.T, clipped)
    new_first = 0.9 * first_moment + 0.1 * rotated
    new_second = 0.95 * second_moment + 0.05 * rotated * rotated
    direction = new_first / (jnp.sqrt(new_second) + 1e-08)
    update = matmul(left_basis, direction)
    new_statistic = 0.95 * left_statistic + 0.05 / D * matmul(clipped, clipped.T)
    power_product = matmul(new_statistic, left_basis)
    iterate = 0.9 * jnp.sqrt(D / (jnp.sum(power_product * power_product) + 1e-06)) * power_product
    for sweep_index in range(NS_STEPS):
        gram_matrix = matmul(iterate.T, iterate)
        iterate = 1.5 * iterate - 0.5 * matmul(iterate, gram_matrix)
    gain_clipped = clip_factor * gain_grad
    new_gain_first = 0.9 * gain_first + 0.1 * gain_clipped
    new_gain_second = 0.95 * gain_second + 0.05 * gain_clipped * gain_clipped
    new_gains = norm_gains - 0.01 * new_gain_first / (jnp.sqrt(new_gain_second) + 1e-08)
    return (update, new_first, new_second, new_statistic, iterate, new_gains, new_gain_first, new_gain_second)
```

```python
import functools
import jax
import jax.numpy as jnp
from jax import lax
from jax.experimental import pallas as pl
from jax.experimental.pallas import tpu as pltpu
from jax.sharding import PartitionSpec as P

D = 2560
NS_STEPS = 3
GROUP = ("tensor", "section")
EVERY = ("shard", "tensor", "section")
PAD = 16

MESH = pl.DeviceIdType.MESH
BF = jnp.bfloat16
F32 = jnp.float32


def nt(a, b):
    return lax.dot_general(a, b, (((1,), (1,)), ((), ())), preferred_element_type=F32)


def nn(a, b):
    return jnp.dot(a, b, preferred_element_type=F32)


def split(v):
    hi = v.astype(BF)
    return hi, (v - hi.astype(F32)).astype(BF)


class Place:
    def __init__(self):
        self.z = z = lax.axis_index("shard")
        self.t = t = lax.axis_index("tensor")
        self.q = q = lax.axis_index("section")
        self.xb, self.yb = q % 2, q // 2
        self.core = (z, 1 - t, q)
        self.xn = (z, t, q + 1 - 2 * self.xb)
        self.yn = (z, t, q + 2 - 4 * self.yb)
        self.up, self.down = (z + 1, t, q), (z - 1, t, q)
        self.peers = [(lax.rem(z + o, 4), t, q) for o in (1, 2, 3)]
        zb = z // 2
        self.order = [z, z + 1 - 2 * (z % 2), 2 - zb, 3 - 3 * zb]

    def greet(self):
        bar = pltpu.get_barrier_semaphore()
        every = [self.core, self.xn, self.yn] + self.peers
        for one in every:
            pl.semaphore_signal(bar, inc=1, device_id=one, device_id_type=MESH)
        pl.semaphore_wait(bar, len(every))


def rcopy(src, dst, ssem, rsem, dev):
    return pltpu.make_async_remote_copy(
        src_ref=src, dst_ref=dst, send_sem=ssem, recv_sem=rsem, device_id=dev, device_id_type=MESH
    )


class LineGather:
    def __init__(self, at, ref, half, zs, zr, cs, cr):
        self.at, self.ref, self.half = at, ref, half
        self.zs, self.zr, self.cs, self.cr = zs, zr, cs, cr

    def part(self, src, own=True):
        t = self.at.t if own else 1 - self.at.t
        return self.ref.at[src, pl.ds(t * self.half, self.half)]

    def along(self, upward, d):
        at = self.at
        src = at.z - (d - 1) if upward else at.z + (d - 1)
        i = d - 1 if upward else 2 + d
        part = self.part(src)
        return rcopy(part, part, self.zs.at[i], self.zr.at[i], at.up if upward else at.down)

    def sends(self, upward, d):
        z = self.at.z
        return jnp.logical_and(z >= d - 1, z <= 2) if upward else jnp.logical_and(z <= 4 - d, z >= 1)

    def comes(self, upward, d):
        return self.at.z >= d if upward else self.at.z + d <= 3

    def across(self, src, i):
        part = self.part(src)
        return rcopy(part, part, self.cs.at[i], self.cr.at[i], self.at.core)

    def arrived(self, src, i, sem):
        part = self.part(src, own=sem is self.zr)
        return rcopy(part, part, self.zs.at[i], sem.at[i], self.at.core)

    def start(self):
        for upward in (True, False):
            @pl.when(self.sends(upward, 1))
            def _():
                self.along(upward, 1).start()
        self.across(self.at.z, 6).start()

    def own(self):
        self.arrived(self.at.z, 6, self.cr).wait_recv()

    def pump(self, d):
        z = self.at.z
        for upward in (True, False):
            i = d - 1 if upward else 2 + d
            @pl.when(self.comes(upward, d))
            def _():
                src = z - d if upward else z + d
                self.arrived(src, i, self.zr).wait_recv()
                if d < 3:
                    @pl.when(self.sends(upward, d + 1))
                    def _():
                        self.along(upward, d + 1).start()
                self.across(src, i).start()

    def land(self, d):
        z = self.at.z
        for upward in (True, False):
            i = d - 1 if upward else 2 + d
            @pl.when(self.comes(upward, d))
            def _():
                self.arrived(z - d if upward else z + d, i, self.cr).wait_recv()

    def finish(self):
        z = self.at.z
        self.across(z, 6).wait_send()
        for d in (1, 2, 3):
            for upward in (True, False):
                i = d - 1 if upward else 2 + d
                @pl.when(self.sends(upward, d))
                def _():
                    self.along(upward, d).wait_send()
                @pl.when(self.comes(upward, d))
                def _():
                    self.across(z - d if upward else z + d, i).wait_send()


class PlaneSum:
    def __init__(self, at, i, acc, r1, r2, eb, ss, rs):
        self.acc, self.r1, self.r2, self.eb = acc, r1, r2, eb
        self.ss, self.rs = ss, rs
        rows = acc.shape[0]
        self.h, self.w = rows // 2, rows // 4
        if i % 2 == 0:
            self.bf, self.bs, self.nf, self.ns = at.xb, at.yb, at.xn, at.yn
        else:
            self.bf, self.bs, self.nf, self.ns = at.yb, at.xb, at.yn, at.xn
        self.k1 = self.h * self.bf
        self.k2 = self.k1 + self.w * self.bs

    def rows1(self):
        return pl.ds(self.k1, self.h)

    def rows2(self):
        return pl.ds(self.k2, self.w)

    def c1(self):
        other = pl.ds(self.h * (1 - self.bf), self.h)
        return rcopy(self.acc.at[other], self.r1, self.ss.at[0], self.rs.at[0], self.nf)

    def c2(self):
        other = pl.ds(self.k1 + self.w * (1 - self.bs), self.w)
        return rcopy(self.acc.at[other], self.r2, self.ss.at[1], self.rs.at[1], self.ns)

    def c3(self):
        part = self.eb.at[self.rows2()]
        return rcopy(part, part, self.ss.at[2], self.rs.at[2], self.ns)

    def c4(self):
        part = self.eb.at[self.rows1()]
        return rcopy(part, part, self.ss.at[3], self.rs.at[3], self.nf)

    def w3(self):
        part = self.eb.at[pl.ds(self.k1 + self.w * (1 - self.bs), self.w)]
        rcopy(part, part, self.ss.at[2], self.rs.at[2], self.ns).wait_recv()

    def w4(self):
        part = self.eb.at[pl.ds(self.h * (1 - self.bf), self.h)]
        rcopy(part, part, self.ss.at[3], self.rs.at[3], self.nf).wait_recv()

    def go1(self):
        self.c1().start()

    def go2(self):
        self.c1().wait_recv()
        self.acc[self.rows1()] = self.acc[self.rows1()] + self.r1[...]
        self.c2().start()

    def total(self):
        self.c2().wait_recv()
        return self.acc[self.rows2()] + self.r2[...]

    def go3(self, value):
        self.eb[self.rows2()] = value.astype(BF)
        self.c3().start()

    def go4(self):
        self.w3()
        self.c4().start()

    def end(self):
        self.w4()

    def finish(self):
        for c in (self.c1(), self.c2(), self.c3(), self.c4()):
            c.wait_send()


def ns_kernel(
    p_ref, out_ref, px, xc, xa, hi, lo, delta, acc, r1, r2, eb, ox, sums, zsums,
    zs, zr, cs, cr, ps, pr, ms, mr,
):
    at = Place()
    z, t = at.z, at.t
    n = p_ref.shape[1]
    half = p_ref.shape[0] // 2
    mine, others = pl.ds(t * half, half), pl.ds((1 - t) * half, half)
    at.greet()
    first = rcopy(p_ref.at[others], px, ms.at[0], mr.at[0], at.core)
    first.start()
    first.wait_recv()
    own, far = p_ref[mine], px[...]
    v = jnp.where(t == 0, jnp.concatenate([own, far], 1), jnp.concatenate([far, own], 1))
    xc[...] = v
    h, l = split(v)
    hi[z, mine] = h
    lo[z, mine] = l
    gathers = [
        [LineGather(at, ref, half, zs.at[g], zr.at[g], cs.at[g], cr.at[g]) for g, ref in pair]
        for pair in ([(0, hi), (1, lo)], [(2, delta.at[0])], [(3, delta.at[1])])
    ]
    for g in gathers[0]:
        g.start()
    sums[0] = jnp.full((8, 128), jnp.sum(v * v), F32)
    stages = [at.core, at.xn, at.yn]

    def norm_copy(j):
        return rcopy(sums.at[2 * j], sums.at[2 * j + 1], ms.at[1 + j], mr.at[1 + j], stages[j])

    def norm_peer(o):
        return rcopy(
            sums.at[6], zsums.at[z], ms.at[4 + o], mr.at[4 + o], at.peers[o]
        )

    def norm_stage(j):
        norm_copy(j).wait_recv()
        sums[2 * j + 2] = sums[2 * j] + sums[2 * j + 1]
        if j < 2:
            norm_copy(j + 1).start()

    norm_copy(0).start()
    scale = None
    for step in range(3):
        sets = gathers[step]
        plane = [
            PlaneSum(at, i, acc.at[step, i], r1.at[step, i], r2.at[step, i], eb.at[step, i],
                     ps.at[step, i], pr.at[step, i])
            for i in range(4)
        ]

        def refresh(src):
            if step == 0:
                return
            old = hi[src].astype(F32) + lo[src].astype(F32)
            if step == 1:
                old = old * scale
            a, b = split(old + delta[step - 1, src].astype(F32))
            hi[src] = a
            lo[src] = b

        def partial(i):
            src = at.order[i]
            refresh(src)
            a, b = hi[z, mine], lo[z, mine]
            acc[step, i] = nt(a, hi[src]) + (nt(a, lo[src]) + nt(b, hi[src]))

        def centred(i):
            total = plane[i].total()
            if step == 0:
                total = total * (scale * scale)
            row = lax.broadcasted_iota(jnp.int32, total.shape, 0)
            col = lax.broadcasted_iota(jnp.int32, total.shape, 1)
            shift = (z - at.order[i]) * (2 * half) + t * half + plane[i].k2
            plane[i].go3(jnp.where(row + shift == col, total - 1.0, total))

        def gather_in(i):
            plane[i].end()
            src = at.order[i]
            e = eb[step, i]
            term = nn(e, hi[src]) + nn(e, lo[src])
            if i == 0:
                xa[...] = term
            else:
                xa[...] += term

        for i in range(4):
            for g in sets:
                if i == 0:
                    g.own()
                else:
                    g.pump(i)
            if i > 0:
                for g in sets:
                    g.land(i)
            partial(i)
            plane[i].go1()
            if step == 0 and i == 0:
                norm_stage(0)
                norm_stage(1)
                norm_stage(2)
                zsums[z] = sums[6]
                for o in range(3):
                    norm_peer(o).start()
                for o in range(3):
                    src = lax.rem(z + 3 - o, 4)
                    rcopy(sums.at[6], zsums.at[src], ms.at[4 + o], mr.at[4 + o], at.peers[o]).wait_recv()
                whole = (zsums[0] + zsums[1]) + (zsums[2] + zsums[3])
                scale = (0.9 * jnp.sqrt(D / (whole + 1e-06)))[0:1, 0:1]
            if i > 0:
                centred(i - 1)
            plane[i].go2()
            if i > 0:
                plane[i - 1].go4()
                if i > 1:
                    gather_in(i - 2)
        centred(3)
        gather_in(2)
        plane[3].go4()
        gather_in(3)
        for g in sets:
            g.finish()
        for p in plane:
            p.finish()
        if step == 0:
            fresh = scale * (xc[...] - 0.5 * xa[...])
        else:
            fresh = xc[...] - 0.5 * xa[...]
        if step < 2:
            xc[...] = fresh
            held = hi[z, mine].astype(F32) + lo[z, mine].astype(F32)
            if step == 0:
                held = held * scale
            delta[step, z, mine] = (fresh - held).astype(BF)
            gathers[step + 1][0].start()
    left, right = fresh[:, :n], fresh[:, n:]
    ox[...] = jnp.where(t == 0, right, left)
    back = rcopy(ox, out_ref.at[mine], ms.at[7], mr.at[7], at.core)
    back.start()
    out_ref[mine] = jnp.where(t == 0, left, right)
    rcopy(ox, out_ref.at[others], ms.at[7], mr.at[7], at.core).wait_recv()
    back.wait_send()
    first.wait_send()
    for j in range(3):
        norm_copy(j).wait_send()
    for o in range(3):
        norm_peer(o).wait_send()


def newton_schulz(p):
    rows, n = p.shape
    half = rows // 2
    dma = pltpu.SemaphoreType.DMA
    return pl.pallas_call(
        ns_kernel,
        out_shape=jax.ShapeDtypeStruct((rows, n), F32),
        in_specs=[pl.BlockSpec(memory_space=pltpu.VMEM)],
        out_specs=pl.BlockSpec(memory_space=pltpu.VMEM),
        scratch_shapes=[
            pltpu.VMEM((half, n), F32),
            pltpu.VMEM((half, 2 * n), F32),
            pltpu.VMEM((half, 2 * n), F32),
            pltpu.VMEM((4, rows, 2 * n), BF),
            pltpu.VMEM((4, rows, 2 * n), BF),
            pltpu.VMEM((2, 4, rows, 2 * n), BF),
            pltpu.VMEM((3, 4, half, rows), F32),
            pltpu.VMEM((3, 4, half // 2, rows), F32),
            pltpu.VMEM((3, 4, half // 4, rows), F32),
            pltpu.VMEM((3, 4, half, rows), BF),
            pltpu.VMEM((half, n), F32),
            pltpu.VMEM((7, 8, 128), F32),
            pltpu.VMEM((4, 8, 128), F32),
            dma((4, 6)), dma((4, 6)), dma((4, 7)), dma((4, 7)),
            dma((3, 4, 4)), dma((3, 4, 4)), dma((8,)), dma((8,)),
        ],
        compiler_params=pltpu.CompilerParams(
            collective_id=7, has_side_effects=True, vmem_limit_bytes=60 << 20
        ),
    )(p)


def matmul(left_side, right_side):
    return jnp.dot(
        left_side, right_side, precision=lax.Precision.HIGH, preferred_element_type=jnp.float32
    )


def row_panel(local_block):
    return lax.all_gather(local_block, GROUP, axis=1, tiled=True)


def same(block):
    return block


def pack(block):
    top = jnp.max(jnp.abs(block), axis=0, keepdims=True)
    power = jnp.clip(jnp.ceil(jnp.log2(jnp.maximum(top, 1e-30))) - 14.0, -110.0, 120.0)
    scaled = block * jnp.exp2(-power)
    tail = jnp.broadcast_to(power, (PAD, block.shape[1]))
    return jnp.concatenate([scaled, tail], axis=0).astype(jnp.float16)


def unpack(payload):
    values = payload.astype(jnp.float32)
    return values[..., :-PAD, :] * jnp.exp2(values[..., -PAD : -PAD + 1, :])


def partners(size):
    if size & (size - 1) == 0:
        return [[(one, one ^ offset) for one in range(size)] for offset in range(1, size)]
    return [
        [(one, (one + offset) % size) for one in range(size)] for offset in range(1, size)
    ]


def place_of_source(place, offset, size):
    return place ^ offset if size & (size - 1) == 0 else (place - offset) % size


def place_of_target(place, offset, size):
    return place ^ offset if size & (size - 1) == 0 else (place + offset) % size


def shard_total(value, shards):
    if shards > 8:
        return lax.psum(value, "shard")
    tile = jnp.full((8, 128), value, jnp.float32)
    total = value
    for pairs in partners(shards):
        total = total + lax.ppermute(tile, "shard", pairs)[0, 0]
    return total


def rows_times_shards(full_rows, block, shards, place, encode, decode):
    if shards > 8:
        gathered = decode(lax.all_gather(encode(block), "shard", axis=0))
        return matmul(full_rows, gathered.reshape(-1, block.shape[1]))
    rows = block.shape[0]
    sent = encode(block)
    pieces = [block] + [
        decode(lax.ppermute(sent, "shard", pairs)) for pairs in partners(shards)
    ]
    total = None
    for offset, piece in enumerate(pieces):
        source = place_of_source(place, offset, shards)
        left = lax.dynamic_slice_in_dim(full_rows, source * rows, rows, 1)
        term = matmul(left, piece)
        total = term if total is None else total + term
    return total


def scatter_product(full_rows, block, shards, place, encode, decode):
    if shards > 8:
        return lax.psum_scatter(
            matmul(full_rows.T, block), "shard", scatter_dimension=0, tiled=True
        )
    rows = full_rows.shape[1] // shards
    arrived = []
    for offset, pairs in enumerate(partners(shards), 1):
        target = place_of_target(place, offset, shards)
        chunk = matmul(lax.dynamic_slice_in_dim(full_rows, target * rows, rows, 1).T, block)
        arrived.append(lax.ppermute(encode(chunk), "shard", pairs))
    total = matmul(lax.dynamic_slice_in_dim(full_rows, place * rows, rows, 1).T, block)
    for payload in arrived:
        total = total + decode(payload)
    return total


def outer_block(gradient, grad_rows, shards, group, place, member):
    rows, cols = gradient.shape
    if rows % cols == 0 and shards <= 8:
        own = lax.dynamic_slice_in_dim(grad_rows, (member * cols) % rows, cols, 0)
        other = jnp.zeros_like(own)
        for offset in range(1, shards):
            pairs = []
            for column in range(group):
                home = column * cols // rows
                pairs.append(
                    (home * group + column, (home + offset) % shards * group + column)
                )
            other = other + lax.ppermute(own, EVERY, pairs)
        partner = jnp.where(place == member * cols // rows, own, other)
        return jnp.dot(grad_rows, partner.T, preferred_element_type=jnp.float32)
    partner = lax.all_gather(gradient, "shard", axis=0, tiled=True)
    product = jnp.dot(gradient, partner.T, preferred_element_type=jnp.float32)
    return lax.psum_scatter(product, GROUP, scatter_dimension=1, tiled=True)


def on_device(
    gradient,
    gain_grad,
    left_statistic,
    left_basis,
    first_moment,
    second_moment,
    norm_gains,
    gain_first,
    gain_second,
):
    group = lax.axis_size(GROUP)
    shards = lax.axis_size("shard")
    place = lax.axis_index("shard")
    member = lax.axis_index(GROUP)
    rows, cols = gradient.shape
    grad_float = gradient.astype(jnp.float32)
    grad_rows = row_panel(gradient)
    late_basis, grad_rows = lax.optimization_barrier((left_basis, grad_rows))
    basis_rows = row_panel(late_basis)
    grad_rows_float = grad_rows.astype(jnp.float32)
    squares_total = shard_total(
        jnp.sum(grad_rows_float * grad_rows_float) + jnp.sum(gain_grad * gain_grad), shards
    )
    clip_factor = jnp.minimum(1.0, D / jnp.sqrt(squares_total + 1e-06))
    outer_part = outer_block(gradient, grad_rows, shards, group, place, member)
    new_statistic = 0.95 * left_statistic + (0.05 / D * clip_factor * clip_factor) * outer_part
    ready_statistic, basis_rows = lax.optimization_barrier((new_statistic, basis_rows))
    statistic_rows = row_panel(ready_statistic)
    power_product = rows_times_shards(
        statistic_rows, left_basis, shards, place, same, same
    )
    fast = (shards, lax.axis_size("tensor"), lax.axis_size("section")) == (4, 2, 4)
    power_rows = None if fast else row_panel(power_product)
    rotated = clip_factor * scatter_product(
        basis_rows, grad_float, shards, place, same, same
    )
    new_first = 0.9 * first_moment + 0.1 * rotated
    new_second = 0.95 * second_moment + 0.05 * rotated * rotated
    direction = new_first / (jnp.sqrt(new_second) + 1e-08)
    update = rows_times_shards(
        basis_rows,
        direction,
        shards,
        place,
        lambda x: x.astype(jnp.float16),
        lambda x: x.astype(jnp.float32),
    )
    if fast:
        iterate = newton_schulz(power_product)
    else:
        update, power_rows = lax.optimization_barrier((update, power_rows))
        power_sum = shard_total(jnp.sum(power_rows * power_rows), shards)
        scale = 0.9 * jnp.sqrt(D / (power_sum + 1e-06))
        iterate = scale * power_product
        iterate_rows = scale * power_rows
        row_index = place * rows + lax.broadcasted_iota(jnp.int32, (rows, cols), 0)
        col_index = member * cols + lax.broadcasted_iota(jnp.int32, (rows, cols), 1)
        eye = (row_index == col_index).astype(jnp.float32)
        for sweep_index in range(NS_STEPS):
            if sweep_index:
                iterate_rows = row_panel(iterate)
                gram_block = scatter_product(
                    iterate_rows, iterate, shards, place, pack, unpack
                )
            else:
                gram_block = (scale * scale) * scatter_product(
                    power_rows, power_product, shards, place, pack, unpack
                )
            iterate = iterate - 0.5 * rows_times_shards(
                iterate_rows, gram_block - eye, shards, place, pack, unpack
            )
    gain_clipped = clip_factor * gain_grad
    new_gain_first = 0.9 * gain_first + 0.1 * gain_clipped
    new_gain_second = 0.95 * gain_second + 0.05 * gain_clipped * gain_clipped
    new_gains = norm_gains - 0.01 * new_gain_first / (jnp.sqrt(new_gain_second) + 1e-08)
    return (
        update,
        new_first,
        new_second,
        new_statistic,
        iterate,
        new_gains,
        new_gain_first,
        new_gain_second,
    )


def solution(mesh):
    matrix = P("shard", GROUP)
    vector = P(None, "shard")
    return jax.shard_map(
        on_device,
        mesh=mesh,
        in_specs=(
            matrix,
            vector,
            matrix,
            matrix,
            matrix,
            matrix,
            vector,
            vector,
            vector,
        ),
        out_specs=(matrix, matrix, matrix, matrix, matrix, vector, vector, vector),
        check_vma=False,
    )
```

```python
import jax
import jax.numpy as jnp
from jax import lax
from jax.experimental import pallas as pl
from jax.experimental.pallas import tpu as pltpu
from jax.sharding import PartitionSpec as P

D = 2560
NS_STEPS = 3
GROUP = ("tensor", "section")
EVERY = ("shard", "tensor", "section")
PAD = 16

MESH = pl.DeviceIdType.MESH
BF = jnp.bfloat16
F32 = jnp.float32


def nt(a, b):
    return lax.dot_general(a, b, (((1,), (1,)), ((), ())), preferred_element_type=F32)


def nn(a, b):
    return jnp.dot(a, b, preferred_element_type=F32)


def tn(a, b):
    return lax.dot_general(a, b, (((0,), (0,)), ((), ())), preferred_element_type=F32)


def split(v):
    hi = v.astype(BF)
    return hi, (v - hi.astype(F32)).astype(BF)


class Place:
    def __init__(self):
        self.z = z = lax.axis_index("shard")
        self.t = t = lax.axis_index("tensor")
        self.q = q = lax.axis_index("section")
        self.xb, self.yb = q % 2, q // 2
        self.core = (z, 1 - t, q)
        self.xn = (z, t, q + 1 - 2 * self.xb)
        self.yn = (z, t, q + 2 - 4 * self.yb)
        self.up, self.down = (z + 1, t, q), (z - 1, t, q)
        self.peers = [(lax.rem(z + o, 4), t, q) for o in (1, 2, 3)]
        zb = z // 2
        self.order = [z, z + 1 - 2 * (z % 2), 2 - zb, 3 - 3 * zb]

    def greet(self):
        bar = pltpu.get_barrier_semaphore()
        every = [self.core, self.xn, self.yn] + self.peers
        for one in every:
            pl.semaphore_signal(bar, inc=1, device_id=one, device_id_type=MESH)
        pl.semaphore_wait(bar, len(every))


def rcopy(src, dst, ssem, rsem, dev):
    return pltpu.make_async_remote_copy(
        src_ref=src, dst_ref=dst, send_sem=ssem, recv_sem=rsem, device_id=dev, device_id_type=MESH
    )


class LineGather:
    def __init__(self, at, ref, half, zs, zr, cs, cr):
        self.at, self.ref, self.half = at, ref, half
        self.zs, self.zr, self.cs, self.cr = zs, zr, cs, cr

    def part(self, src, own=True):
        t = self.at.t if own else 1 - self.at.t
        return self.ref.at[src, pl.ds(t * self.half, self.half)]

    def along(self, upward, d):
        at = self.at
        src = at.z - (d - 1) if upward else at.z + (d - 1)
        i = d - 1 if upward else 2 + d
        part = self.part(src)
        return rcopy(part, part, self.zs.at[i], self.zr.at[i], at.up if upward else at.down)

    def sends(self, upward, d):
        z = self.at.z
        return jnp.logical_and(z >= d - 1, z <= 2) if upward else jnp.logical_and(z <= 4 - d, z >= 1)

    def comes(self, upward, d):
        return self.at.z >= d if upward else self.at.z + d <= 3

    def across(self, src, i):
        part = self.part(src)
        return rcopy(part, part, self.cs.at[i], self.cr.at[i], self.at.core)

    def arrived(self, src, i, sem):
        part = self.part(src, own=sem is self.zr)
        return rcopy(part, part, self.zs.at[i], sem.at[i], self.at.core)

    def start(self):
        for upward in (True, False):
            @pl.when(self.sends(upward, 1))
            def _():
                self.along(upward, 1).start()
        self.across(self.at.z, 6).start()

    def own(self):
        self.arrived(self.at.z, 6, self.cr).wait_recv()

    def pump(self, d):
        z = self.at.z
        for upward in (True, False):
            i = d - 1 if upward else 2 + d
            @pl.when(self.comes(upward, d))
            def _():
                src = z - d if upward else z + d
                self.arrived(src, i, self.zr).wait_recv()
                if d < 3:
                    @pl.when(self.sends(upward, d + 1))
                    def _():
                        self.along(upward, d + 1).start()
                self.across(src, i).start()

    def land(self, d):
        z = self.at.z
        for upward in (True, False):
            i = d - 1 if upward else 2 + d
            @pl.when(self.comes(upward, d))
            def _():
                self.arrived(z - d if upward else z + d, i, self.cr).wait_recv()

    def finish(self):
        z = self.at.z
        self.across(z, 6).wait_send()
        for d in (1, 2, 3):
            for upward in (True, False):
                i = d - 1 if upward else 2 + d
                @pl.when(self.sends(upward, d))
                def _():
                    self.along(upward, d).wait_send()
                @pl.when(self.comes(upward, d))
                def _():
                    self.across(z - d if upward else z + d, i).wait_send()


class PlaneSum:
    def __init__(self, at, x_first, base, rows, acc, r1, r2, eb, ss, rs):
        self.acc, self.eb = acc, eb
        self.ss, self.rs = ss, rs
        self.base, self.h, self.w = base, rows // 2, rows // 4
        self.r1, self.r2 = r1.at[pl.ds(base // 2, self.h)], r2.at[pl.ds(base // 4, self.w)]
        if x_first:
            self.bf, self.bs, self.nf, self.ns = at.xb, at.yb, at.xn, at.yn
        else:
            self.bf, self.bs, self.nf, self.ns = at.yb, at.xb, at.yn, at.xn
        self.k1 = base + self.h * self.bf
        self.k2 = self.k1 + self.w * self.bs

    def back(self, rows):
        return self.eb.at[:, rows] if len(self.eb.shape) == 3 else self.eb.at[rows]

    def rows1(self):
        return pl.ds(self.k1, self.h)

    def rows2(self):
        return pl.ds(self.k2, self.w)

    def c1(self):
        other = pl.ds(self.base + self.h * (1 - self.bf), self.h)
        return rcopy(self.acc.at[other], self.r1, self.ss.at[0], self.rs.at[0], self.nf)

    def c2(self):
        other = pl.ds(self.k1 + self.w * (1 - self.bs), self.w)
        return rcopy(self.acc.at[other], self.r2, self.ss.at[1], self.rs.at[1], self.ns)

    def c3(self):
        part = self.back(self.rows2())
        return rcopy(part, part, self.ss.at[2], self.rs.at[2], self.ns)

    def c4(self):
        part = self.back(self.rows1())
        return rcopy(part, part, self.ss.at[3], self.rs.at[3], self.nf)

    def w3(self):
        part = self.back(pl.ds(self.k1 + self.w * (1 - self.bs), self.w))
        rcopy(part, part, self.ss.at[2], self.rs.at[2], self.ns).wait_recv()

    def w4(self):
        part = self.back(pl.ds(self.base + self.h * (1 - self.bf), self.h))
        rcopy(part, part, self.ss.at[3], self.rs.at[3], self.nf).wait_recv()

    def go1(self):
        self.c1().start()

    def go2(self):
        self.c1().wait_recv()
        self.acc[self.rows1()] = self.acc[self.rows1()] + self.r1[...]
        self.c2().start()

    def total(self):
        self.c2().wait_recv()
        return self.acc[self.rows2()] + self.r2[...]

    def go3(self, value):
        if len(self.eb.shape) == 3:
            high, low = split(value)
            self.eb[0, self.rows2()] = high
            self.eb[1, self.rows2()] = low
        else:
            self.eb[self.rows2()] = value.astype(BF)
        self.c3().start()

    def go4(self):
        self.w3()
        self.c4().start()

    def end(self):
        self.w4()

    def finish(self):
        for c in (self.c1(), self.c2(), self.c3(), self.c4()):
            c.wait_send()


class GlobalSum:
    def __init__(self, at, sums, zsums, ss, rs):
        self.at, self.sums, self.zsums, self.ss, self.rs = at, sums, zsums, ss, rs
        self.stages = [at.core, at.xn, at.yn]

    def near(self, j):
        return rcopy(self.sums.at[2 * j], self.sums.at[2 * j + 1], self.ss.at[j], self.rs.at[j], self.stages[j])

    def far(self, o, src):
        return rcopy(self.sums.at[6], self.zsums.at[src], self.ss.at[3 + o], self.rs.at[3 + o], self.at.peers[o])

    def start(self, value):
        self.sums[0] = jnp.full((8, 128), value, F32)
        self.near(0).start()

    def result(self):
        z, sums, zsums = self.at.z, self.sums, self.zsums
        for j in range(3):
            self.near(j).wait_recv()
            sums[2 * j + 2] = sums[2 * j] + sums[2 * j + 1]
            if j < 2:
                self.near(j + 1).start()
        zsums[z] = sums[6]
        for o in range(3):
            self.far(o, z).start()
        for o in range(3):
            self.far(o, lax.rem(z + 3 - o, 4)).wait_recv()
        return (zsums[0] + zsums[1]) + (zsums[2] + zsums[3])

    def finish(self):
        for j in range(3):
            self.near(j).wait_send()
        for o in range(3):
            self.far(o, self.at.z).wait_send()


def side_by_side(t, own, far):
    return jnp.where(t == 0, jnp.concatenate([own, far], 1), jnp.concatenate([far, own], 1))


def cuts(rows, i):
    large = rows // 2 + 32
    first = large if i % 2 == 0 else rows - large
    return [(0, first), (first, rows - first)]


def ns_kernel(
    p_ref, out_ref, xc, xa, hi, lo, delta, acc, r1, r2, eb, ox, sums, zsums,
    zs, zr, cs, cr, ps, pr, ms, mr,
):
    at = Place()
    z, t = at.z, at.t
    half, n = p_ref.shape[0], p_ref.shape[1] // 2
    mine, others = pl.ds(t * half, half), pl.ds((1 - t) * half, half)
    at.greet()
    v = p_ref[...]
    xc[...] = v
    h, l = split(v)
    hi[z, mine] = h
    lo[z, mine] = l
    gathers = [
        [LineGather(at, ref, half, zs.at[g], zr.at[g], cs.at[g], cr.at[g]) for g, ref in pair]
        for pair in ([(0, hi), (1, lo)], [(2, delta.at[0])], [(3, delta.at[1])])
    ]
    for g in gathers[0]:
        g.start()
    norm = GlobalSum(at, sums, zsums, ms, mr)
    norm.start(jnp.sum(v * v))
    scale = None
    for step in range(3):
        sets = gathers[step]
        plane = [
            [
                PlaneSum(at, side == 0, base, size, acc.at[step, i], r1.at[step, i], r2.at[step, i],
                         eb.at[step, i], ps.at[step, i, side], pr.at[step, i, side])
                for side, (base, size) in enumerate(cuts(half, i))
            ]
            for i in range(4)
        ]

        def refresh(src):
            if step == 0:
                return
            old = hi[src].astype(F32) + lo[src].astype(F32)
            if step == 1:
                old = old * scale
            a, b = split(old + delta[step - 1, src].astype(F32))
            hi[src] = a
            lo[src] = b

        def partial(i):
            src = at.order[i]
            refresh(src)
            a, b = hi[z, mine], lo[z, mine]
            acc[step, i] = nt(a, hi[src]) + (nt(a, lo[src]) + nt(b, hi[src]))

        def centred(i):
            for p in plane[i]:
                total = p.total()
                if step == 0:
                    total = total * (scale * scale)
                row = lax.broadcasted_iota(jnp.int32, total.shape, 0)
                col = lax.broadcasted_iota(jnp.int32, total.shape, 1)
                shift = (z - at.order[i]) * (2 * half) + t * half + p.k2
                p.go3(jnp.where(row + shift == col, total - 1.0, total))

        def gather_in(i):
            for p in plane[i]:
                p.end()
            src = at.order[i]
            e = eb[step, i]
            term = nn(e, hi[src]) + nn(e, lo[src])
            if i == 0:
                xa[...] = term
            else:
                xa[...] += term

        for i in range(4):
            for g in sets:
                if i == 0:
                    g.own()
                else:
                    g.pump(i)
            if i > 0:
                for g in sets:
                    g.land(i)
            partial(i)
            for p in plane[i]:
                p.go1()
            if step == 0 and i == 0:
                whole = norm.result()
                scale = (0.9 * jnp.sqrt(D / (whole + 1e-06)))[0:1, 0:1]
            if i > 0:
                centred(i - 1)
            for p in plane[i]:
                p.go2()
            if i > 0:
                for p in plane[i - 1]:
                    p.go4()
                if i > 1:
                    gather_in(i - 2)
        centred(3)
        gather_in(2)
        for p in plane[3]:
            p.go4()
        gather_in(3)
        for g in sets:
            g.finish()
        for pair in plane:
            for p in pair:
                p.finish()
        if step == 0:
            fresh = scale * (xc[...] - 0.5 * xa[...])
        else:
            fresh = xc[...] - 0.5 * xa[...]
        if step < 2:
            xc[...] = fresh
            held = hi[z, mine].astype(F32) + lo[z, mine].astype(F32)
            if step == 0:
                held = held * scale
            delta[step, z, mine] = (fresh - held).astype(BF)
            gathers[step + 1][0].start()
    left, right = fresh[:, :n], fresh[:, n:]
    ox[...] = jnp.where(t == 0, right, left)
    back = rcopy(ox, out_ref.at[mine], ms.at[7], mr.at[7], at.core)
    back.start()
    out_ref[mine] = jnp.where(t == 0, left, right)
    rcopy(ox, out_ref.at[others], ms.at[7], mr.at[7], at.core).wait_recv()
    back.wait_send()
    norm.finish()


def front_kernel(
    g_ref, l_ref, b_ref, gain_ref, power_ref, stat_ref, rot_ref, clip_ref, gx, lx, bx, lpad, gall, hi, lo,
    bc, ra, oy, bs, br,
    acc, r1, r2, eb, ox, sums, zsums, zs, zr, cs, cr, ps, pr, ms, mr, xs, xr,
):
    at = Place()
    z, t = at.z, at.t
    n = g_ref.shape[1]
    half = g_ref.shape[0] // 2
    mine, others = pl.ds(t * half, half), pl.ds((1 - t) * half, half)
    at.greet()
    swaps = [
        rcopy(ref.at[others], dst, xs.at[i], xr.at[i], at.core)
        for i, (ref, dst) in enumerate([(g_ref, gx), (b_ref, bx), (l_ref, lx)])
    ]
    for one in swaps:
        one.start()
    grads = LineGather(at, gall, half, zs.at[0], zr.at[0], cs.at[0], cr.at[0])
    bases = [
        LineGather(at, ref, half, zs.at[1 + i], zr.at[1 + i], cs.at[1 + i], cr.at[1 + i])
        for i, ref in enumerate([hi, lo])
    ]
    swaps[0].wait_recv()
    gall[z, mine] = side_by_side(t, g_ref[mine], gx[...])
    grads.start()
    gf = g_ref[...].astype(F32)
    norm = GlobalSum(at, sums, zsums, ms, mr)
    norm.start(jnp.sum(gf * gf) + jnp.sum(gain_ref[...] * gain_ref[...]) * 0.125)
    swaps[1].wait_recv()
    h, l = split(side_by_side(t, b_ref[mine], bx[...]))
    hi[z, mine] = h
    lo[z, mine] = l
    swaps[2].wait_recv()
    own, far = l_ref[mine], lx[...]
    zero = jnp.zeros_like(own)
    for j in range(2):
        block = jnp.where(t == j, own, far)
        lpad[j] = side_by_side(at.xb, block, zero)
    whole = norm.result()
    clip = jnp.minimum(1.0, D / jnp.sqrt(whole + 1e-06))
    clip_ref[...] = clip
    coef = (0.05 / D * clip * clip)[0:1, 0:1]
    plane = [
        [
            PlaneSum(at, side == 0, base, size, acc.at[i], r1.at[i], r2.at[i],
                     eb.at[at.order[i]], ps.at[i, side], pr.at[i, side])
            for side, (base, size) in enumerate(cuts(half, i))
        ]
        for i in range(4)
    ]

    def partial(i):
        src = at.order[i]
        mix = jnp.where(src % 2 == at.yb, 0.95, 0.0).astype(F32)
        acc[i] = coef * nt(gall[z, mine], gall[src]) + mix * lpad[src // 2]

    def centred(i):
        for p in plane[i]:
            p.go3(p.total())

    for i in range(4):
        if i == 0:
            grads.own()
        else:
            grads.pump(i)
            if i == 2:
                for b in bases:
                    b.start()
            grads.land(i)
        partial(i)
        for p in plane[i]:
            p.go1()
        if i > 0:
            centred(i - 1)
        for p in plane[i]:
            p.go2()
        if i > 0:
            for p in plane[i - 1]:
                p.go4()
    near_x, near_y = at.xb == t, at.yb == z % 2
    origin = jnp.logical_and(near_x, near_y)
    relay = jnp.logical_and(near_x, jnp.logical_not(near_y))

    def spread(i, axis):
        part = bc.at[at.order[i]]
        return rcopy(part, part, bs.at[axis, i], br.at[axis, i], at.yn if axis else at.xn)

    def spread_start(i):
        src = at.order[i]

        @pl.when(origin)
        def _():
            for j, ref in enumerate((hi, lo)):
                v = ref[src].astype(F32)
                bc[src, j] = jnp.where(z < 2, v[:, :n], v[:, n:]).astype(BF)
            spread(i, 1).start()
            spread(i, 0).start()

    def spread_relay(i):
        @pl.when(relay)
        def _():
            spread(i, 1).wait_recv()
            spread(i, 0).start()

    def rotate(i):
        @pl.when(jnp.logical_not(near_x))
        def _():
            spread(i, 0).wait_recv()

        src = at.order[i]
        term = tn(bc[src, 0], gall[src]) + tn(bc[src, 1], gall[src])
        if i == 0:
            ra[...] = term
        else:
            ra[...] += term

    for b in bases:
        b.own()
    centred(3)
    for b in bases:
        b.pump(1)
    for p in plane[3]:
        p.go4()
    for i in range(4):
        for p in plane[i]:
            p.end()
        if i > 0:
            for b in bases:
                if i > 1:
                    b.pump(i)
                b.land(i)
        spread_start(i)
        src = at.order[i]
        sh, sl = eb[src, 0], eb[src, 1]
        term = nn(sh, hi[src]) + (nn(sh, lo[src]) + nn(sl, hi[src]))
        if i == 0:
            power_ref[...] = term
        else:
            power_ref[...] += term
            spread_relay(i - 1)
        if i > 1:
            rotate(i - 2)
    spread_relay(3)
    for j, place in ((0, t), (1, 1 - t)):
        c = 2 * place + at.yb
        v = eb[c, 0].astype(F32) + eb[c, 1].astype(F32)
        v = jnp.where(at.xb == 0, v[:, :n], v[:, n:])
        if j == 0:
            stat_ref[mine] = v
        else:
            ox[...] = v
    back = rcopy(ox, stat_ref.at[mine], xs.at[3], xr.at[3], at.core)
    back.start()
    rotate(2)
    rotate(3)
    turned = clip[0:1, 0:1] * ra[...]
    oy[...] = jnp.where(t == 0, turned[:, n:], turned[:, :n])
    rot_back = rcopy(oy, rot_ref.at[mine], xs.at[4], xr.at[4], at.core)
    rot_back.start()
    rot_ref[mine] = jnp.where(t == 0, turned[:, :n], turned[:, n:])
    rcopy(ox, stat_ref.at[others], xs.at[3], xr.at[3], at.core).wait_recv()
    rcopy(oy, rot_ref.at[others], xs.at[4], xr.at[4], at.core).wait_recv()
    back.wait_send()
    rot_back.wait_send()
    for i in range(4):
        @pl.when(near_x)
        def _():
            spread(i, 0).wait_send()

        @pl.when(origin)
        def _():
            spread(i, 1).wait_send()

    grads.finish()
    for b in bases:
        b.finish()
    for pair in plane:
        for p in pair:
            p.finish()
    norm.finish()
    for one in swaps:
        one.wait_send()


def front(gradient, statistic, basis, gain):
    rows, n = gradient.shape
    half = rows // 2
    dma = pltpu.SemaphoreType.DMA
    vmem = pl.BlockSpec(memory_space=pltpu.VMEM)
    return pl.pallas_call(
        front_kernel,
        out_shape=(
            jax.ShapeDtypeStruct((half, 2 * n), F32),
            jax.ShapeDtypeStruct((rows, n), F32),
            jax.ShapeDtypeStruct((rows, n), F32),
            jax.ShapeDtypeStruct((8, 128), F32),
        ),
        in_specs=[vmem] * 4,
        out_specs=(vmem,) * 4,
        cost_estimate=pl.CostEstimate(flops=10**11, bytes_accessed=4 * 10**8, transcendentals=0),
        scratch_shapes=[
            pltpu.VMEM((half, n), BF),
            pltpu.VMEM((half, n), F32),
            pltpu.VMEM((half, n), F32),
            pltpu.VMEM((2, half, 2 * n), F32),
            pltpu.VMEM((4, rows, 2 * n), BF),
            pltpu.VMEM((4, rows, 2 * n), BF),
            pltpu.VMEM((4, rows, 2 * n), BF),
            pltpu.VMEM((4, 2, rows, n), BF),
            pltpu.VMEM((half, 2 * n), F32),
            pltpu.VMEM((half, n), F32),
            dma((2, 4)), dma((2, 4)),
            pltpu.VMEM((4, half, rows), F32),
            pltpu.VMEM((4, half // 2, rows), F32),
            pltpu.VMEM((4, half // 4, rows), F32),
            pltpu.VMEM((4, 2, half, rows), BF),
            pltpu.VMEM((half, n), F32),
            pltpu.VMEM((7, 8, 128), F32),
            pltpu.VMEM((4, 8, 128), F32),
            dma((3, 6)), dma((3, 6)), dma((3, 7)), dma((3, 7)),
            dma((4, 2, 4)), dma((4, 2, 4)), dma((8,)), dma((8,)), dma((5,)), dma((5,)),
        ],
        compiler_params=pltpu.CompilerParams(
            collective_id=8, has_side_effects=True, vmem_limit_bytes=56 << 20
        ),
    )(gradient, statistic, basis, gain)


def newton_schulz(p):
    half, rows = p.shape
    n = rows // 2
    rows = 2 * half
    dma = pltpu.SemaphoreType.DMA
    return pl.pallas_call(
        ns_kernel,
        out_shape=jax.ShapeDtypeStruct((rows, n), F32),
        in_specs=[pl.BlockSpec(memory_space=pltpu.VMEM)],
        out_specs=pl.BlockSpec(memory_space=pltpu.VMEM),
        cost_estimate=pl.CostEstimate(flops=10**11, bytes_accessed=10**9, transcendentals=0),
        scratch_shapes=[
            pltpu.VMEM((half, 2 * n), F32),
            pltpu.VMEM((half, 2 * n), F32),
            pltpu.VMEM((4, rows, 2 * n), BF),
            pltpu.VMEM((4, rows, 2 * n), BF),
            pltpu.VMEM((2, 4, rows, 2 * n), BF),
            pltpu.VMEM((3, 4, half, rows), F32),
            pltpu.VMEM((3, 4, half // 2, rows), F32),
            pltpu.VMEM((3, 4, half // 4, rows), F32),
            pltpu.VMEM((3, 4, half, rows), BF),
            pltpu.VMEM((half, n), F32),
            pltpu.VMEM((7, 8, 128), F32),
            pltpu.VMEM((4, 8, 128), F32),
            dma((4, 6)), dma((4, 6)), dma((4, 7)), dma((4, 7)),
            dma((3, 4, 2, 4)), dma((3, 4, 2, 4)), dma((8,)), dma((8,)),
        ],
        compiler_params=pltpu.CompilerParams(
            collective_id=7, has_side_effects=True, vmem_limit_bytes=60 << 20
        ),
    )(p)


def matmul(left_side, right_side):
    return jnp.dot(
        left_side, right_side, precision=lax.Precision.HIGH, preferred_element_type=jnp.float32
    )


def row_panel(local_block):
    return lax.all_gather(local_block, GROUP, axis=1, tiled=True)


def same(block):
    return block


def pack(block):
    top = jnp.max(jnp.abs(block), axis=0, keepdims=True)
    power = jnp.clip(jnp.ceil(jnp.log2(jnp.maximum(top, 1e-30))) - 14.0, -110.0, 120.0)
    scaled = block * jnp.exp2(-power)
    tail = jnp.broadcast_to(power, (PAD, block.shape[1]))
    return jnp.concatenate([scaled, tail], axis=0).astype(jnp.float16)


def unpack(payload):
    values = payload.astype(jnp.float32)
    return values[..., :-PAD, :] * jnp.exp2(values[..., -PAD : -PAD + 1, :])


def partners(size):
    if size & (size - 1) == 0:
        return [[(one, one ^ offset) for one in range(size)] for offset in range(1, size)]
    return [
        [(one, (one + offset) % size) for one in range(size)] for offset in range(1, size)
    ]


def place_of_source(place, offset, size):
    return place ^ offset if size & (size - 1) == 0 else (place - offset) % size


def place_of_target(place, offset, size):
    return place ^ offset if size & (size - 1) == 0 else (place + offset) % size


def shard_total(value, shards):
    if shards > 8:
        return lax.psum(value, "shard")
    tile = jnp.full((8, 128), value, jnp.float32)
    total = value
    for pairs in partners(shards):
        total = total + lax.ppermute(tile, "shard", pairs)[0, 0]
    return total


def rows_times_shards(full_rows, block, shards, place, encode, decode):
    if shards > 8:
        gathered = decode(lax.all_gather(encode(block), "shard", axis=0))
        return matmul(full_rows, gathered.reshape(-1, block.shape[1]))
    rows = block.shape[0]
    sent = encode(block)
    pieces = [block] + [
        decode(lax.ppermute(sent, "shard", pairs)) for pairs in partners(shards)
    ]
    total = None
    for offset, piece in enumerate(pieces):
        source = place_of_source(place, offset, shards)
        left = lax.dynamic_slice_in_dim(full_rows, source * rows, rows, 1)
        term = matmul(left, piece)
        total = term if total is None else total + term
    return total


def scatter_product(full_rows, block, shards, place, encode, decode):
    if shards > 8:
        return lax.psum_scatter(
            matmul(full_rows.T, block), "shard", scatter_dimension=0, tiled=True
        )
    rows = full_rows.shape[1] // shards
    arrived = []
    for offset, pairs in enumerate(partners(shards), 1):
        target = place_of_target(place, offset, shards)
        chunk = matmul(lax.dynamic_slice_in_dim(full_rows, target * rows, rows, 1).T, block)
        arrived.append(lax.ppermute(encode(chunk), "shard", pairs))
    total = matmul(lax.dynamic_slice_in_dim(full_rows, place * rows, rows, 1).T, block)
    for payload in arrived:
        total = total + decode(payload)
    return total


def outer_block(gradient, grad_rows, shards, group, place, member):
    rows, cols = gradient.shape
    if rows % cols == 0 and shards <= 8:
        own = lax.dynamic_slice_in_dim(grad_rows, (member * cols) % rows, cols, 0)
        other = jnp.zeros_like(own)
        for offset in range(1, shards):
            pairs = []
            for column in range(group):
                home = column * cols // rows
                pairs.append(
                    (home * group + column, (home + offset) % shards * group + column)
                )
            other = other + lax.ppermute(own, EVERY, pairs)
        partner = jnp.where(place == member * cols // rows, own, other)
        return jnp.dot(grad_rows, partner.T, preferred_element_type=jnp.float32)
    partner = lax.all_gather(gradient, "shard", axis=0, tiled=True)
    product = jnp.dot(gradient, partner.T, preferred_element_type=jnp.float32)
    return lax.psum_scatter(product, GROUP, scatter_dimension=1, tiled=True)


def plain(
    gradient,
    gain_grad,
    left_statistic,
    left_basis,
    first_moment,
    second_moment,
    norm_gains,
    gain_first,
    gain_second,
):
    group = lax.axis_size(GROUP)
    shards = lax.axis_size("shard")
    place = lax.axis_index("shard")
    member = lax.axis_index(GROUP)
    rows, cols = gradient.shape
    grad_float = gradient.astype(jnp.float32)
    grad_rows = row_panel(gradient)
    late_basis, grad_rows = lax.optimization_barrier((left_basis, grad_rows))
    basis_rows = row_panel(late_basis)
    grad_rows_float = grad_rows.astype(jnp.float32)
    squares_total = shard_total(
        jnp.sum(grad_rows_float * grad_rows_float) + jnp.sum(gain_grad * gain_grad), shards
    )
    clip_factor = jnp.minimum(1.0, D / jnp.sqrt(squares_total + 1e-06))
    outer_part = outer_block(gradient, grad_rows, shards, group, place, member)
    new_statistic = 0.95 * left_statistic + (0.05 / D * clip_factor * clip_factor) * outer_part
    ready_statistic, basis_rows = lax.optimization_barrier((new_statistic, basis_rows))
    statistic_rows = row_panel(ready_statistic)
    power_product = rows_times_shards(
        statistic_rows, left_basis, shards, place, same, same
    )
    power_rows = row_panel(power_product)
    rotated = clip_factor * scatter_product(
        basis_rows, grad_float, shards, place, same, same
    )
    new_first = 0.9 * first_moment + 0.1 * rotated
    new_second = 0.95 * second_moment + 0.05 * rotated * rotated
    direction = new_first / (jnp.sqrt(new_second) + 1e-08)
    update = rows_times_shards(
        basis_rows,
        direction,
        shards,
        place,
        lambda x: x.astype(jnp.float16),
        lambda x: x.astype(jnp.float32),
    )
    update, power_rows = lax.optimization_barrier((update, power_rows))
    power_sum = shard_total(jnp.sum(power_rows * power_rows), shards)
    scale = 0.9 * jnp.sqrt(D / (power_sum + 1e-06))
    iterate = scale * power_product
    iterate_rows = scale * power_rows
    row_index = place * rows + lax.broadcasted_iota(jnp.int32, (rows, cols), 0)
    col_index = member * cols + lax.broadcasted_iota(jnp.int32, (rows, cols), 1)
    eye = (row_index == col_index).astype(jnp.float32)
    for sweep_index in range(NS_STEPS):
        if sweep_index:
            iterate_rows = row_panel(iterate)
            gram_block = scatter_product(
                iterate_rows, iterate, shards, place, pack, unpack
            )
        else:
            gram_block = (scale * scale) * scatter_product(
                power_rows, power_product, shards, place, pack, unpack
            )
        iterate = iterate - 0.5 * rows_times_shards(
            iterate_rows, gram_block - eye, shards, place, pack, unpack
        )
    gain_clipped = clip_factor * gain_grad
    new_gain_first = 0.9 * gain_first + 0.1 * gain_clipped
    new_gain_second = 0.95 * gain_second + 0.05 * gain_clipped * gain_clipped
    new_gains = norm_gains - 0.01 * new_gain_first / (jnp.sqrt(new_gain_second) + 1e-08)
    return (
        update,
        new_first,
        new_second,
        new_statistic,
        iterate,
        new_gains,
        new_gain_first,
        new_gain_second,
    )


def fast(
    gradient,
    gain_grad,
    left_statistic,
    left_basis,
    first_moment,
    second_moment,
    norm_gains,
    gain_first,
    gain_second,
):
    shards = lax.axis_size("shard")
    place = lax.axis_index("shard")
    power, new_statistic, rotated, clip_tile = front(
        gradient, left_statistic, left_basis, gain_grad
    )
    clip_factor = clip_tile[0, 0]
    power, rotated, late_basis = lax.optimization_barrier((power, rotated, left_basis))
    basis_rows = row_panel(late_basis)
    new_first = 0.9 * first_moment + 0.1 * rotated
    new_second = 0.95 * second_moment + 0.05 * rotated * rotated
    direction = new_first / (jnp.sqrt(new_second) + 1e-08)
    new_basis = newton_schulz(power)
    update = rows_times_shards(
        basis_rows,
        direction,
        shards,
        place,
        lambda x: x.astype(jnp.float16),
        lambda x: x.astype(jnp.float32),
    )
    gain_clipped = clip_factor * gain_grad
    new_gain_first = 0.9 * gain_first + 0.1 * gain_clipped
    new_gain_second = 0.95 * gain_second + 0.05 * gain_clipped * gain_clipped
    new_gains = norm_gains - 0.01 * new_gain_first / (jnp.sqrt(new_gain_second) + 1e-08)
    return (
        update,
        new_first,
        new_second,
        new_statistic,
        new_basis,
        new_gains,
        new_gain_first,
        new_gain_second,
    )


def solution(mesh):
    sizes = tuple(mesh.shape[name] for name in EVERY)
    on_device = fast if sizes == (4, 2, 4) else plain
    matrix = P("shard", GROUP)
    vector = P(None, "shard")
    return jax.shard_map(
        on_device,
        mesh=mesh,
        in_specs=(
            matrix,
            vector,
            matrix,
            matrix,
            matrix,
            matrix,
            vector,
            vector,
            vector,
        ),
        out_specs=(matrix, matrix, matrix, matrix, matrix, vector, vector, vector),
        check_vma=False,
    )
```

```python
import jax
import jax.numpy as jnp
from jax import lax
from jax.experimental import pallas as pl
from jax.experimental.pallas import tpu as pltpu
from jax.sharding import PartitionSpec as P

D = 2560
NS_STEPS = 3
GROUP = ("tensor", "section")
EVERY = ("shard", "tensor", "section")
PAD = 16

MESH = pl.DeviceIdType.MESH
BF = jnp.bfloat16
F32 = jnp.float32


def nt(a, b):
    return lax.dot_general(a, b, (((1,), (1,)), ((), ())), preferred_element_type=F32)


def nn(a, b):
    return jnp.dot(a, b, preferred_element_type=F32)


def tn(a, b):
    return lax.dot_general(a, b, (((0,), (0,)), ((), ())), preferred_element_type=F32)


def split(v):
    hi = v.astype(BF)
    return hi, (v - hi.astype(F32)).astype(BF)


class Place:
    def __init__(self):
        self.z = z = lax.axis_index("shard")
        self.t = t = lax.axis_index("tensor")
        self.q = q = lax.axis_index("section")
        self.xb, self.yb = q % 2, q // 2
        self.core = (z, 1 - t, q)
        self.xn = (z, t, q + 1 - 2 * self.xb)
        self.yn = (z, t, q + 2 - 4 * self.yb)
        self.up, self.down = (z + 1, t, q), (z - 1, t, q)
        self.peers = [(lax.rem(z + o, 4), t, q) for o in (1, 2, 3)]
        zb = z // 2
        self.order = [z, z + 1 - 2 * (z % 2), 2 - zb, 3 - 3 * zb]

    def greet(self):
        bar = pltpu.get_barrier_semaphore()
        every = [self.core, self.xn, self.yn] + self.peers
        for one in every:
            pl.semaphore_signal(bar, inc=1, device_id=one, device_id_type=MESH)
        pl.semaphore_wait(bar, len(every))


def rcopy(src, dst, ssem, rsem, dev):
    return pltpu.make_async_remote_copy(
        src_ref=src, dst_ref=dst, send_sem=ssem, recv_sem=rsem, device_id=dev, device_id_type=MESH
    )


class LineGather:
    def __init__(self, at, ref, half, zs, zr, cs, cr):
        self.at, self.ref, self.half = at, ref, half
        self.zs, self.zr, self.cs, self.cr = zs, zr, cs, cr

    def part(self, src, own=True):
        t = self.at.t if own else 1 - self.at.t
        return self.ref.at[src, pl.ds(t * self.half, self.half)]

    def along(self, upward, d):
        at = self.at
        src = at.z - (d - 1) if upward else at.z + (d - 1)
        i = d - 1 if upward else 2 + d
        part = self.part(src)
        return rcopy(part, part, self.zs.at[i], self.zr.at[i], at.up if upward else at.down)

    def sends(self, upward, d):
        z = self.at.z
        return jnp.logical_and(z >= d - 1, z <= 2) if upward else jnp.logical_and(z <= 4 - d, z >= 1)

    def comes(self, upward, d):
        return self.at.z >= d if upward else self.at.z + d <= 3

    def across(self, src, i):
        part = self.part(src)
        return rcopy(part, part, self.cs.at[i], self.cr.at[i], self.at.core)

    def arrived(self, src, i, sem):
        part = self.part(src, own=sem is self.zr)
        return rcopy(part, part, self.zs.at[i], sem.at[i], self.at.core)

    def start(self):
        for upward in (True, False):
            @pl.when(self.sends(upward, 1))
            def _():
                self.along(upward, 1).start()
        self.across(self.at.z, 6).start()

    def own(self):
        self.arrived(self.at.z, 6, self.cr).wait_recv()

    def pump(self, d):
        z = self.at.z
        for upward in (True, False):
            i = d - 1 if upward else 2 + d
            @pl.when(self.comes(upward, d))
            def _():
                src = z - d if upward else z + d
                self.arrived(src, i, self.zr).wait_recv()
                if d < 3:
                    @pl.when(self.sends(upward, d + 1))
                    def _():
                        self.along(upward, d + 1).start()
                self.across(src, i).start()

    def land(self, d):
        z = self.at.z
        for upward in (True, False):
            i = d - 1 if upward else 2 + d
            @pl.when(self.comes(upward, d))
            def _():
                self.arrived(z - d if upward else z + d, i, self.cr).wait_recv()

    def finish(self):
        z = self.at.z
        self.across(z, 6).wait_send()
        for d in (1, 2, 3):
            for upward in (True, False):
                i = d - 1 if upward else 2 + d
                @pl.when(self.sends(upward, d))
                def _():
                    self.along(upward, d).wait_send()
                @pl.when(self.comes(upward, d))
                def _():
                    self.across(z - d if upward else z + d, i).wait_send()


class LineMoves(LineGather):
    def __init__(self, at, src_ref, ref, zs, zr):
        self.at, self.first, self.ref, self.zs, self.zr = at, src_ref, ref, zs, zr

    def along(self, upward, d):
        at = self.at
        src = at.z - (d - 1) if upward else at.z + (d - 1)
        i = d - 1 if upward else 2 + d
        part = self.ref.at[src]
        return rcopy(
            self.first if d == 1 else part, part, self.zs.at[i], self.zr.at[i],
            at.up if upward else at.down,
        )

    def start(self):
        for upward in (True, False):
            @pl.when(self.sends(upward, 1))
            def _():
                self.along(upward, 1).start()

    def pump(self, d):
        z = self.at.z
        for upward in (True, False):
            i = d - 1 if upward else 2 + d
            @pl.when(self.comes(upward, d))
            def _():
                part = self.ref.at[z - d if upward else z + d]
                rcopy(part, part, self.zs.at[i], self.zr.at[i], self.at.core).wait_recv()
                if d < 3:
                    @pl.when(self.sends(upward, d + 1))
                    def _():
                        self.along(upward, d + 1).start()

    def finish(self):
        for d in (1, 2, 3):
            for upward in (True, False):
                @pl.when(self.sends(upward, d))
                def _():
                    self.along(upward, d).wait_send()


class PlaneSum:
    def __init__(self, at, x_first, base, rows, acc, r1, r2, eb, ss, rs):
        self.acc, self.eb = acc, eb
        self.ss, self.rs = ss, rs
        self.base, self.h, self.w = base, rows // 2, rows // 4
        self.r1, self.r2 = r1.at[pl.ds(base // 2, self.h)], r2.at[pl.ds(base // 4, self.w)]
        if x_first:
            self.bf, self.bs, self.nf, self.ns = at.xb, at.yb, at.xn, at.yn
        else:
            self.bf, self.bs, self.nf, self.ns = at.yb, at.xb, at.yn, at.xn
        self.k1 = base + self.h * self.bf
        self.k2 = self.k1 + self.w * self.bs

    def back(self, rows):
        return self.eb.at[:, rows] if len(self.eb.shape) == 3 else self.eb.at[rows]

    def rows1(self):
        return pl.ds(self.k1, self.h)

    def rows2(self):
        return pl.ds(self.k2, self.w)

    def c1(self):
        other = pl.ds(self.base + self.h * (1 - self.bf), self.h)
        return rcopy(self.acc.at[other], self.r1, self.ss.at[0], self.rs.at[0], self.nf)

    def c2(self):
        other = pl.ds(self.k1 + self.w * (1 - self.bs), self.w)
        return rcopy(self.acc.at[other], self.r2, self.ss.at[1], self.rs.at[1], self.ns)

    def c3(self):
        part = self.back(self.rows2())
        return rcopy(part, part, self.ss.at[2], self.rs.at[2], self.ns)

    def c4(self):
        part = self.back(self.rows1())
        return rcopy(part, part, self.ss.at[3], self.rs.at[3], self.nf)

    def w3(self):
        part = self.back(pl.ds(self.k1 + self.w * (1 - self.bs), self.w))
        rcopy(part, part, self.ss.at[2], self.rs.at[2], self.ns).wait_recv()

    def w4(self):
        part = self.back(pl.ds(self.base + self.h * (1 - self.bf), self.h))
        rcopy(part, part, self.ss.at[3], self.rs.at[3], self.nf).wait_recv()

    def go1(self):
        self.c1().start()

    def go2(self):
        self.c1().wait_recv()
        self.acc[self.rows1()] = self.acc[self.rows1()] + self.r1[...]
        self.c2().start()

    def total(self):
        self.c2().wait_recv()
        return self.acc[self.rows2()] + self.r2[...]

    def go3(self, value):
        if len(self.eb.shape) == 3:
            high, low = split(value)
            self.eb[0, self.rows2()] = high
            self.eb[1, self.rows2()] = low
        else:
            self.eb[self.rows2()] = value.astype(BF)
        self.c3().start()

    def go4(self):
        self.w3()
        self.c4().start()

    def end(self):
        self.w4()

    def finish(self):
        for c in (self.c1(), self.c2(), self.c3(), self.c4()):
            c.wait_send()


class GlobalSum:
    def __init__(self, at, sums, zsums, ss, rs):
        self.at, self.sums, self.zsums, self.ss, self.rs = at, sums, zsums, ss, rs
        self.stages = [at.core, at.xn, at.yn]

    def near(self, j):
        return rcopy(self.sums.at[2 * j], self.sums.at[2 * j + 1], self.ss.at[j], self.rs.at[j], self.stages[j])

    def far(self, o, src):
        return rcopy(self.sums.at[6], self.zsums.at[src], self.ss.at[3 + o], self.rs.at[3 + o], self.at.peers[o])

    def start(self, value):
        self.sums[0] = jnp.full((8, 128), value, F32)
        self.near(0).start()

    def result(self):
        z, sums, zsums = self.at.z, self.sums, self.zsums
        for j in range(3):
            self.near(j).wait_recv()
            sums[2 * j + 2] = sums[2 * j] + sums[2 * j + 1]
            if j < 2:
                self.near(j + 1).start()
        zsums[z] = sums[6]
        for o in range(3):
            self.far(o, z).start()
        for o in range(3):
            self.far(o, lax.rem(z + 3 - o, 4)).wait_recv()
        return (zsums[0] + zsums[1]) + (zsums[2] + zsums[3])

    def finish(self):
        for j in range(3):
            self.near(j).wait_send()
        for o in range(3):
            self.far(o, self.at.z).wait_send()


def side_by_side(t, own, far):
    return jnp.where(t == 0, jnp.concatenate([own, far], 1), jnp.concatenate([far, own], 1))


def cuts(rows, i):
    large = rows // 2 + 32
    first = large if i % 2 == 0 else rows - large
    return [(0, first), (first, rows - first)]


def ns_kernel(
    p_ref, d_ref, out_ref, all_ref, xc, xa, hi, lo, delta, acc, r1, r2, eb, ox, sums, zsums,
    zs, zr, cs, cr, ps, pr, ms, mr, ds, dr, own_sem,
):
    at = Place()
    z, t = at.z, at.t
    half, n = p_ref.shape[0], p_ref.shape[1] // 2
    mine, others = pl.ds(t * half, half), pl.ds((1 - t) * half, half)
    at.greet()
    keep = pltpu.make_async_copy(d_ref, all_ref.at[z], own_sem)
    keep.start()
    moves = LineMoves(at, d_ref, all_ref, ds, dr)
    v = p_ref[...]
    xc[...] = v
    h, l = split(v)
    hi[z, mine] = h
    lo[z, mine] = l
    gathers = [
        [LineGather(at, ref, half, zs.at[g], zr.at[g], cs.at[g], cr.at[g]) for g, ref in pair]
        for pair in ([(0, hi), (1, lo)], [(2, delta.at[0])], [(3, delta.at[1])])
    ]
    for g in gathers[0]:
        g.start()
    norm = GlobalSum(at, sums, zsums, ms, mr)
    norm.start(jnp.sum(v * v))
    scale = None
    for step in range(3):
        sets = gathers[step]
        plane = [
            [
                PlaneSum(at, side == 0, base, size, acc.at[step, i], r1.at[step, i], r2.at[step, i],
                         eb.at[step, i], ps.at[step, i, side], pr.at[step, i, side])
                for side, (base, size) in enumerate(cuts(half, i))
            ]
            for i in range(4)
        ]

        def refresh(src):
            if step == 0:
                return
            old = hi[src].astype(F32) + lo[src].astype(F32)
            if step == 1:
                old = old * scale
            a, b = split(old + delta[step - 1, src].astype(F32))
            hi[src] = a
            lo[src] = b

        def partial(i):
            src = at.order[i]
            refresh(src)
            a, b = hi[z, mine], lo[z, mine]
            acc[step, i] = nt(a, hi[src]) + (nt(a, lo[src]) + nt(b, hi[src]))

        def centred(i):
            for p in plane[i]:
                total = p.total()
                if step == 0:
                    total = total * (scale * scale)
                row = lax.broadcasted_iota(jnp.int32, total.shape, 0)
                col = lax.broadcasted_iota(jnp.int32, total.shape, 1)
                shift = (z - at.order[i]) * (2 * half) + t * half + p.k2
                p.go3(jnp.where(row + shift == col, total - 1.0, total))

        def gather_in(i):
            for p in plane[i]:
                p.end()
            src = at.order[i]
            e = eb[step, i]
            term = nn(e, hi[src]) + nn(e, lo[src])
            if i == 0:
                xa[...] = term
            else:
                xa[...] += term

        for i in range(4):
            for g in sets:
                if i == 0:
                    g.own()
                else:
                    g.pump(i)
            if i > 1:
                for p in plane[i - 2]:
                    p.go4()
            if i > 0:
                for g in sets:
                    g.land(i)
                for p in plane[i - 1]:
                    p.go2()
            partial(i)
            for p in plane[i]:
                p.go1()
            if step == 0 and i == 0:
                whole = norm.result()
                scale = (0.9 * jnp.sqrt(D / (whole + 1e-06)))[0:1, 0:1]
            if i > 0:
                centred(i - 1)
            if i > 2:
                gather_in(i - 3)
        if step == 0:
            moves.start()
        else:
            moves.pump(step)
        for p in plane[2]:
            p.go4()
        gather_in(1)
        for p in plane[3]:
            p.go2()
        centred(3)
        gather_in(2)
        for p in plane[3]:
            p.go4()
        gather_in(3)
        for g in sets:
            g.finish()
        for pair in plane:
            for p in pair:
                p.finish()
        if step == 0:
            fresh = scale * (xc[...] - 0.5 * xa[...])
        else:
            fresh = xc[...] - 0.5 * xa[...]
        if step < 2:
            xc[...] = fresh
            held = hi[z, mine].astype(F32) + lo[z, mine].astype(F32)
            if step == 0:
                held = held * scale
            delta[step, z, mine] = (fresh - held).astype(BF)
            gathers[step + 1][0].start()
    left, right = fresh[:, :n], fresh[:, n:]
    ox[...] = jnp.where(t == 0, right, left)
    back = rcopy(ox, out_ref.at[mine], ms.at[7], mr.at[7], at.core)
    back.start()
    out_ref[mine] = jnp.where(t == 0, left, right)
    rcopy(ox, out_ref.at[others], ms.at[7], mr.at[7], at.core).wait_recv()
    back.wait_send()
    moves.pump(3)
    moves.finish()
    keep.wait()
    norm.finish()


def front_kernel(
    g_ref, l_ref, b_ref, gain_ref, power_ref, stat_ref, rot_ref, clip_ref, gx, lx, bx, lpad, gall, hi, lo,
    bc, ra, oy, bs, br,
    acc, r1, r2, eb, ox, sums, zsums, zs, zr, cs, cr, ps, pr, ms, mr, xs, xr,
):
    at = Place()
    z, t = at.z, at.t
    n = g_ref.shape[1]
    half = g_ref.shape[0] // 2
    mine, others = pl.ds(t * half, half), pl.ds((1 - t) * half, half)
    at.greet()
    swaps = [
        rcopy(ref.at[others], dst, xs.at[i], xr.at[i], at.core)
        for i, (ref, dst) in enumerate([(g_ref, gx), (b_ref, bx), (l_ref, lx)])
    ]
    for one in swaps:
        one.start()
    grads = LineGather(at, gall, half, zs.at[0], zr.at[0], cs.at[0], cr.at[0])
    bases = [
        LineGather(at, ref, half, zs.at[1 + i], zr.at[1 + i], cs.at[1 + i], cr.at[1 + i])
        for i, ref in enumerate([hi, lo])
    ]
    swaps[0].wait_recv()
    gall[z, mine] = side_by_side(t, g_ref[mine], gx[...])
    grads.start()
    gf = g_ref[...].astype(F32)
    norm = GlobalSum(at, sums, zsums, ms, mr)
    norm.start(jnp.sum(gf * gf) + jnp.sum(gain_ref[...] * gain_ref[...]) * 0.125)
    swaps[1].wait_recv()
    h, l = split(side_by_side(t, b_ref[mine], bx[...]))
    hi[z, mine] = h
    lo[z, mine] = l
    swaps[2].wait_recv()
    own, far = l_ref[mine], lx[...]
    zero = jnp.zeros_like(own)
    for j in range(2):
        block = jnp.where(t == j, own, far)
        lpad[j] = side_by_side(at.xb, block, zero)
    whole = norm.result()
    clip = jnp.minimum(1.0, D / jnp.sqrt(whole + 1e-06))
    clip_ref[...] = clip
    coef = (0.05 / D * clip * clip)[0:1, 0:1]
    plane = [
        [
            PlaneSum(at, side == 0, base, size, acc.at[i], r1.at[i], r2.at[i],
                     eb.at[at.order[i]], ps.at[i, side], pr.at[i, side])
            for side, (base, size) in enumerate(cuts(half, i))
        ]
        for i in range(4)
    ]

    def partial(i):
        src = at.order[i]
        mix = jnp.where(src % 2 == at.yb, 0.95, 0.0).astype(F32)
        acc[i] = coef * nt(gall[z, mine], gall[src]) + mix * lpad[src // 2]

    def centred(i):
        for p in plane[i]:
            p.go3(p.total())

    near_x, near_y = at.xb == t, at.yb == z % 2
    origin = jnp.logical_and(near_x, near_y)
    relay = jnp.logical_and(near_x, jnp.logical_not(near_y))

    def spread(i, axis, j):
        part = bc.at[at.order[i], j]
        return rcopy(part, part, bs.at[axis, i, j], br.at[axis, i, j], at.yn if axis else at.xn)

    def spread_start(i):
        src = at.order[i]

        @pl.when(origin)
        def _():
            for j, ref in enumerate((hi, lo)):
                v = ref[src].astype(F32)
                bc[src, j] = jnp.where(z < 2, v[:, :n], v[:, n:]).astype(BF)
                spread(i, 1, j).start()
                spread(i, 0, j).start()

    def spread_relay(i):
        @pl.when(relay)
        def _():
            for j in range(2):
                spread(i, 1, j).wait_recv()
                spread(i, 0, j).start()

    def rotate(i):
        @pl.when(jnp.logical_not(near_x))
        def _():
            for j in range(2):
                spread(i, 0, j).wait_recv()

        src = at.order[i]
        term = tn(bc[src, 0], gall[src]) + tn(bc[src, 1], gall[src])
        if i == 0:
            ra[...] = term
        else:
            ra[...] += term

    for i in range(4):
        if i == 0:
            grads.own()
        else:
            grads.pump(i)
            if i == 1:
                for b in bases:
                    b.start()
            if i > 1:
                for p in plane[i - 2]:
                    p.go4()
            grads.land(i)
            for p in plane[i - 1]:
                p.go2()
        partial(i)
        for p in plane[i]:
            p.go1()
        if i > 0:
            centred(i - 1)
        if i == 1:
            for b in bases:
                b.own()
            spread_start(0)
        if i == 3:
            spread_relay(0)
    for p in plane[2]:
        p.go4()
    for b in bases:
        b.pump(1)
    for p in plane[3]:
        p.go2()
    centred(3)
    for b in bases:
        b.land(1)
    spread_start(1)
    for p in plane[3]:
        p.go4()
    rotate(0)
    for i in range(4):
        for p in plane[i]:
            p.end()
        if i > 1:
            for b in bases:
                b.pump(i)
            for b in bases:
                b.land(i)
            spread_start(i)
        src = at.order[i]
        sh, sl = eb[src, 0], eb[src, 1]
        term = nn(sh, hi[src]) + (nn(sh, lo[src]) + nn(sl, hi[src]))
        if i == 0:
            power_ref[...] = term
        else:
            power_ref[...] += term
        if i > 1:
            spread_relay(i - 1)
        if i > 2:
            rotate(i - 2)
    spread_relay(3)
    for j, place in ((0, t), (1, 1 - t)):
        c = 2 * place + at.yb
        v = eb[c, 0].astype(F32) + eb[c, 1].astype(F32)
        v = jnp.where(at.xb == 0, v[:, :n], v[:, n:])
        if j == 0:
            stat_ref[mine] = v
        else:
            ox[...] = v
    back = rcopy(ox, stat_ref.at[mine], xs.at[3], xr.at[3], at.core)
    back.start()
    rotate(2)
    rotate(3)
    turned = clip[0:1, 0:1] * ra[...]
    oy[...] = jnp.where(t == 0, turned[:, n:], turned[:, :n])
    rot_back = rcopy(oy, rot_ref.at[mine], xs.at[4], xr.at[4], at.core)
    rot_back.start()
    rot_ref[mine] = jnp.where(t == 0, turned[:, :n], turned[:, n:])
    rcopy(ox, stat_ref.at[others], xs.at[3], xr.at[3], at.core).wait_recv()
    rcopy(oy, rot_ref.at[others], xs.at[4], xr.at[4], at.core).wait_recv()
    back.wait_send()
    rot_back.wait_send()
    for i in range(4):
        @pl.when(near_x)
        def _():
            for j in range(2):
                spread(i, 0, j).wait_send()

        @pl.when(origin)
        def _():
            for j in range(2):
                spread(i, 1, j).wait_send()

    grads.finish()
    for b in bases:
        b.finish()
    for pair in plane:
        for p in pair:
            p.finish()
    norm.finish()
    for one in swaps:
        one.wait_send()


def front(gradient, statistic, basis, gain):
    rows, n = gradient.shape
    half = rows // 2
    dma = pltpu.SemaphoreType.DMA
    vmem = pl.BlockSpec(memory_space=pltpu.VMEM)
    return pl.pallas_call(
        front_kernel,
        out_shape=(
            jax.ShapeDtypeStruct((half, 2 * n), F32),
            jax.ShapeDtypeStruct((rows, n), F32),
            jax.ShapeDtypeStruct((rows, n), F32),
            jax.ShapeDtypeStruct((8, 128), F32),
        ),
        in_specs=[vmem] * 4,
        out_specs=(vmem,) * 4,
        cost_estimate=pl.CostEstimate(flops=10**11, bytes_accessed=4 * 10**8, transcendentals=0),
        scratch_shapes=[
            pltpu.VMEM((half, n), BF),
            pltpu.VMEM((half, n), F32),
            pltpu.VMEM((half, n), F32),
            pltpu.VMEM((2, half, 2 * n), F32),
            pltpu.VMEM((4, rows, 2 * n), BF),
            pltpu.VMEM((4, rows, 2 * n), BF),
            pltpu.VMEM((4, rows, 2 * n), BF),
            pltpu.VMEM((4, 2, rows, n), BF),
            pltpu.VMEM((half, 2 * n), F32),
            pltpu.VMEM((half, n), F32),
            dma((2, 4, 2)), dma((2, 4, 2)),
            pltpu.VMEM((4, half, rows), F32),
            pltpu.VMEM((4, half // 2, rows), F32),
            pltpu.VMEM((4, half // 4, rows), F32),
            pltpu.VMEM((4, 2, half, rows), BF),
            pltpu.VMEM((half, n), F32),
            pltpu.VMEM((7, 8, 128), F32),
            pltpu.VMEM((4, 8, 128), F32),
            dma((3, 6)), dma((3, 6)), dma((3, 7)), dma((3, 7)),
            dma((4, 2, 4)), dma((4, 2, 4)), dma((8,)), dma((8,)), dma((5,)), dma((5,)),
        ],
        compiler_params=pltpu.CompilerParams(
            collective_id=8, has_side_effects=True, vmem_limit_bytes=56 << 20
        ),
    )(gradient, statistic, basis, gain)


def newton_schulz(p, extra):
    half, rows = p.shape
    n = rows // 2
    rows = 2 * half
    dma = pltpu.SemaphoreType.DMA
    return pl.pallas_call(
        ns_kernel,
        out_shape=(
            jax.ShapeDtypeStruct((rows, n), F32),
            jax.ShapeDtypeStruct((4, *extra.shape), extra.dtype),
        ),
        in_specs=[pl.BlockSpec(memory_space=pltpu.VMEM), pl.BlockSpec(memory_space=pl.ANY)],
        out_specs=(pl.BlockSpec(memory_space=pltpu.VMEM), pl.BlockSpec(memory_space=pl.ANY)),
        cost_estimate=pl.CostEstimate(flops=10**11, bytes_accessed=10**9, transcendentals=0),
        scratch_shapes=[
            pltpu.VMEM((half, 2 * n), F32),
            pltpu.VMEM((half, 2 * n), F32),
            pltpu.VMEM((4, rows, 2 * n), BF),
            pltpu.VMEM((4, rows, 2 * n), BF),
            pltpu.VMEM((2, 4, rows, 2 * n), BF),
            pltpu.VMEM((3, 4, half, rows), F32),
            pltpu.VMEM((3, 4, half // 2, rows), F32),
            pltpu.VMEM((3, 4, half // 4, rows), F32),
            pltpu.VMEM((3, 4, half, rows), BF),
            pltpu.VMEM((half, n), F32),
            pltpu.VMEM((7, 8, 128), F32),
            pltpu.VMEM((4, 8, 128), F32),
            dma((4, 6)), dma((4, 6)), dma((4, 7)), dma((4, 7)),
            dma((3, 4, 2, 4)), dma((3, 4, 2, 4)), dma((8,)), dma((8,)),
            dma((6,)), dma((6,)), dma(()),
        ],
        compiler_params=pltpu.CompilerParams(
            collective_id=7, has_side_effects=True, vmem_limit_bytes=60 << 20
        ),
    )(p, extra)


def matmul(left_side, right_side):
    return jnp.dot(
        left_side, right_side, precision=lax.Precision.HIGH, preferred_element_type=jnp.float32
    )


def row_panel(local_block):
    return lax.all_gather(local_block, GROUP, axis=1, tiled=True)


def same(block):
    return block


def pack(block):
    top = jnp.max(jnp.abs(block), axis=0, keepdims=True)
    power = jnp.clip(jnp.ceil(jnp.log2(jnp.maximum(top, 1e-30))) - 14.0, -110.0, 120.0)
    scaled = block * jnp.exp2(-power)
    tail = jnp.broadcast_to(power, (PAD, block.shape[1]))
    return jnp.concatenate([scaled, tail], axis=0).astype(jnp.float16)


def unpack(payload):
    values = payload.astype(jnp.float32)
    return values[..., :-PAD, :] * jnp.exp2(values[..., -PAD : -PAD + 1, :])


def partners(size):
    if size & (size - 1) == 0:
        return [[(one, one ^ offset) for one in range(size)] for offset in range(1, size)]
    return [
        [(one, (one + offset) % size) for one in range(size)] for offset in range(1, size)
    ]


def place_of_source(place, offset, size):
    return place ^ offset if size & (size - 1) == 0 else (place - offset) % size


def place_of_target(place, offset, size):
    return place ^ offset if size & (size - 1) == 0 else (place + offset) % size


def shard_total(value, shards):
    if shards > 8:
        return lax.psum(value, "shard")
    tile = jnp.full((8, 128), value, jnp.float32)
    total = value
    for pairs in partners(shards):
        total = total + lax.ppermute(tile, "shard", pairs)[0, 0]
    return total


def rows_times_shards(full_rows, block, shards, place, encode, decode):
    if shards > 8:
        gathered = decode(lax.all_gather(encode(block), "shard", axis=0))
        return matmul(full_rows, gathered.reshape(-1, block.shape[1]))
    rows = block.shape[0]
    sent = encode(block)
    pieces = [block] + [
        decode(lax.ppermute(sent, "shard", pairs)) for pairs in partners(shards)
    ]
    total = None
    for offset, piece in enumerate(pieces):
        source = place_of_source(place, offset, shards)
        left = lax.dynamic_slice_in_dim(full_rows, source * rows, rows, 1)
        term = matmul(left, piece)
        total = term if total is None else total + term
    return total


def scatter_product(full_rows, block, shards, place, encode, decode):
    if shards > 8:
        return lax.psum_scatter(
            matmul(full_rows.T, block), "shard", scatter_dimension=0, tiled=True
        )
    rows = full_rows.shape[1] // shards
    arrived = []
    for offset, pairs in enumerate(partners(shards), 1):
        target = place_of_target(place, offset, shards)
        chunk = matmul(lax.dynamic_slice_in_dim(full_rows, target * rows, rows, 1).T, block)
        arrived.append(lax.ppermute(encode(chunk), "shard", pairs))
    total = matmul(lax.dynamic_slice_in_dim(full_rows, place * rows, rows, 1).T, block)
    for payload in arrived:
        total = total + decode(payload)
    return total


def outer_block(gradient, grad_rows, shards, group, place, member):
    rows, cols = gradient.shape
    if rows % cols == 0 and shards <= 8:
        own = lax.dynamic_slice_in_dim(grad_rows, (member * cols) % rows, cols, 0)
        other = jnp.zeros_like(own)
        for offset in range(1, shards):
            pairs = []
            for column in range(group):
                home = column * cols // rows
                pairs.append(
                    (home * group + column, (home + offset) % shards * group + column)
                )
            other = other + lax.ppermute(own, EVERY, pairs)
        partner = jnp.where(place == member * cols // rows, own, other)
        return jnp.dot(grad_rows, partner.T, preferred_element_type=jnp.float32)
    partner = lax.all_gather(gradient, "shard", axis=0, tiled=True)
    product = jnp.dot(gradient, partner.T, preferred_element_type=jnp.float32)
    return lax.psum_scatter(product, GROUP, scatter_dimension=1, tiled=True)


def plain(
    gradient,
    gain_grad,
    left_statistic,
    left_basis,
    first_moment,
    second_moment,
    norm_gains,
    gain_first,
    gain_second,
):
    group = lax.axis_size(GROUP)
    shards = lax.axis_size("shard")
    place = lax.axis_index("shard")
    member = lax.axis_index(GROUP)
    rows, cols = gradient.shape
    grad_float = gradient.astype(jnp.float32)
    grad_rows = row_panel(gradient)
    late_basis, grad_rows = lax.optimization_barrier((left_basis, grad_rows))
    basis_rows = row_panel(late_basis)
    grad_rows_float = grad_rows.astype(jnp.float32)
    squares_total = shard_total(
        jnp.sum(grad_rows_float * grad_rows_float) + jnp.sum(gain_grad * gain_grad), shards
    )
    clip_factor = jnp.minimum(1.0, D / jnp.sqrt(squares_total + 1e-06))
    outer_part = outer_block(gradient, grad_rows, shards, group, place, member)
    new_statistic = 0.95 * left_statistic + (0.05 / D * clip_factor * clip_factor) * outer_part
    ready_statistic, basis_rows = lax.optimization_barrier((new_statistic, basis_rows))
    statistic_rows = row_panel(ready_statistic)
    power_product = rows_times_shards(
        statistic_rows, left_basis, shards, place, same, same
    )
    power_rows = row_panel(power_product)
    rotated = clip_factor * scatter_product(
        basis_rows, grad_float, shards, place, same, same
    )
    new_first = 0.9 * first_moment + 0.1 * rotated
    new_second = 0.95 * second_moment + 0.05 * rotated * rotated
    direction = new_first / (jnp.sqrt(new_second) + 1e-08)
    update = rows_times_shards(
        basis_rows,
        direction,
        shards,
        place,
        lambda x: x.astype(jnp.float16),
        lambda x: x.astype(jnp.float32),
    )
    update, power_rows = lax.optimization_barrier((update, power_rows))
    power_sum = shard_total(jnp.sum(power_rows * power_rows), shards)
    scale = 0.9 * jnp.sqrt(D / (power_sum + 1e-06))
    iterate = scale * power_product
    iterate_rows = scale * power_rows
    row_index = place * rows + lax.broadcasted_iota(jnp.int32, (rows, cols), 0)
    col_index = member * cols + lax.broadcasted_iota(jnp.int32, (rows, cols), 1)
    eye = (row_index == col_index).astype(jnp.float32)
    for sweep_index in range(NS_STEPS):
        if sweep_index:
            iterate_rows = row_panel(iterate)
            gram_block = scatter_product(
                iterate_rows, iterate, shards, place, pack, unpack
            )
        else:
            gram_block = (scale * scale) * scatter_product(
                power_rows, power_product, shards, place, pack, unpack
            )
        iterate = iterate - 0.5 * rows_times_shards(
            iterate_rows, gram_block - eye, shards, place, pack, unpack
        )
    gain_clipped = clip_factor * gain_grad
    new_gain_first = 0.9 * gain_first + 0.1 * gain_clipped
    new_gain_second = 0.95 * gain_second + 0.05 * gain_clipped * gain_clipped
    new_gains = norm_gains - 0.01 * new_gain_first / (jnp.sqrt(new_gain_second) + 1e-08)
    return (
        update,
        new_first,
        new_second,
        new_statistic,
        iterate,
        new_gains,
        new_gain_first,
        new_gain_second,
    )


def fast(
    gradient,
    gain_grad,
    left_statistic,
    left_basis,
    first_moment,
    second_moment,
    norm_gains,
    gain_first,
    gain_second,
):
    power, new_statistic, rotated, clip_tile = front(
        gradient, left_statistic, left_basis, gain_grad
    )
    clip_factor = clip_tile[0, 0]
    power, rotated, late_basis = lax.optimization_barrier((power, rotated, left_basis))
    basis_rows = row_panel(late_basis)
    new_first = 0.9 * first_moment + 0.1 * rotated
    new_second = 0.95 * second_moment + 0.05 * rotated * rotated
    direction = new_first / (jnp.sqrt(new_second) + 1e-08)
    new_basis, all_rows = newton_schulz(power, direction)
    update = matmul(basis_rows, all_rows.reshape(-1, direction.shape[1]))
    gain_clipped = clip_factor * gain_grad
    new_gain_first = 0.9 * gain_first + 0.1 * gain_clipped
    new_gain_second = 0.95 * gain_second + 0.05 * gain_clipped * gain_clipped
    new_gains = norm_gains - 0.01 * new_gain_first / (jnp.sqrt(new_gain_second) + 1e-08)
    return (
        update,
        new_first,
        new_second,
        new_statistic,
        new_basis,
        new_gains,
        new_gain_first,
        new_gain_second,
    )


def solution(mesh):
    sizes = tuple(mesh.shape[name] for name in EVERY)
    on_device = fast if sizes == (4, 2, 4) else plain
    matrix = P("shard", GROUP)
    vector = P(None, "shard")
    return jax.shard_map(
        on_device,
        mesh=mesh,
        in_specs=(
            matrix,
            vector,
            matrix,
            matrix,
            matrix,
            matrix,
            vector,
            vector,
            vector,
        ),
        out_specs=(matrix, matrix, matrix, matrix, matrix, vector, vector, vector),
        check_vma=False,
    )
```

```python
import jax
import jax.numpy as jnp
from jax import lax
from jax.experimental import pallas as pl
from jax.experimental.pallas import tpu as pltpu
from jax.sharding import PartitionSpec as P

D = 2560
NS_STEPS = 3
GROUP = ("tensor", "section")
EVERY = ("shard", "tensor", "section")
PAD = 16

MESH = pl.DeviceIdType.MESH
BF = jnp.bfloat16
F32 = jnp.float32


def nt(a, b):
    return lax.dot_general(a, b, (((1,), (1,)), ((), ())), preferred_element_type=F32)


def nn(a, b):
    return jnp.dot(a, b, preferred_element_type=F32)


def tn(a, b):
    return lax.dot_general(a, b, (((0,), (0,)), ((), ())), preferred_element_type=F32)


def split(v):
    hi = v.astype(BF)
    return hi, (v - hi.astype(F32)).astype(BF)


class Place:
    def __init__(self):
        self.z = z = lax.axis_index("shard")
        self.t = t = lax.axis_index("tensor")
        self.q = q = lax.axis_index("section")
        self.xb, self.yb = q % 2, q // 2
        self.core = (z, 1 - t, q)
        self.xn = (z, t, q + 1 - 2 * self.xb)
        self.yn = (z, t, q + 2 - 4 * self.yb)
        self.up, self.down = (z + 1, t, q), (z - 1, t, q)
        self.peers = [(lax.rem(z + o, 4), t, q) for o in (1, 2, 3)]
        zb = z // 2
        self.order = [z, z + 1 - 2 * (z % 2), 2 - zb, 3 - 3 * zb]

    def greet(self):
        bar = pltpu.get_barrier_semaphore()
        every = [self.core, self.xn, self.yn] + self.peers
        for one in every:
            pl.semaphore_signal(bar, inc=1, device_id=one, device_id_type=MESH)
        pl.semaphore_wait(bar, len(every))


def rcopy(src, dst, ssem, rsem, dev):
    return pltpu.make_async_remote_copy(
        src_ref=src, dst_ref=dst, send_sem=ssem, recv_sem=rsem, device_id=dev, device_id_type=MESH
    )


class LineGather:
    def __init__(self, at, ref, half, zs, zr, cs, cr):
        self.at, self.ref, self.half = at, ref, half
        self.zs, self.zr, self.cs, self.cr = zs, zr, cs, cr

    def part(self, src, own=True):
        t = self.at.t if own else 1 - self.at.t
        return self.ref.at[src, pl.ds(t * self.half, self.half)]

    def along(self, upward, d):
        at = self.at
        src = at.z - (d - 1) if upward else at.z + (d - 1)
        i = d - 1 if upward else 2 + d
        part = self.part(src)
        return rcopy(part, part, self.zs.at[i], self.zr.at[i], at.up if upward else at.down)

    def sends(self, upward, d):
        z = self.at.z
        return jnp.logical_and(z >= d - 1, z <= 2) if upward else jnp.logical_and(z <= 4 - d, z >= 1)

    def comes(self, upward, d):
        return self.at.z >= d if upward else self.at.z + d <= 3

    def across(self, src, i):
        part = self.part(src)
        return rcopy(part, part, self.cs.at[i], self.cr.at[i], self.at.core)

    def arrived(self, src, i, sem):
        part = self.part(src, own=sem is self.zr)
        return rcopy(part, part, self.zs.at[i], sem.at[i], self.at.core)

    def start(self):
        for upward in (True, False):
            @pl.when(self.sends(upward, 1))
            def _():
                self.along(upward, 1).start()
        self.across(self.at.z, 6).start()

    def own(self):
        self.arrived(self.at.z, 6, self.cr).wait_recv()

    def pump(self, d):
        z = self.at.z
        for upward in (True, False):
            i = d - 1 if upward else 2 + d
            @pl.when(self.comes(upward, d))
            def _():
                src = z - d if upward else z + d
                self.arrived(src, i, self.zr).wait_recv()
                if d < 3:
                    @pl.when(self.sends(upward, d + 1))
                    def _():
                        self.along(upward, d + 1).start()
                self.across(src, i).start()

    def land(self, d):
        z = self.at.z
        for upward in (True, False):
            i = d - 1 if upward else 2 + d
            @pl.when(self.comes(upward, d))
            def _():
                self.arrived(z - d if upward else z + d, i, self.cr).wait_recv()

    def finish(self):
        z = self.at.z
        self.across(z, 6).wait_send()
        for d in (1, 2, 3):
            for upward in (True, False):
                i = d - 1 if upward else 2 + d
                @pl.when(self.sends(upward, d))
                def _():
                    self.along(upward, d).wait_send()
                @pl.when(self.comes(upward, d))
                def _():
                    self.across(z - d if upward else z + d, i).wait_send()


class LineMoves(LineGather):
    def __init__(self, at, src_ref, ref, zs, zr):
        self.at, self.first, self.ref, self.zs, self.zr = at, src_ref, ref, zs, zr

    def along(self, upward, d):
        at = self.at
        src = at.z - (d - 1) if upward else at.z + (d - 1)
        i = d - 1 if upward else 2 + d
        part = self.ref.at[src]
        return rcopy(
            self.first if d == 1 else part, part, self.zs.at[i], self.zr.at[i],
            at.up if upward else at.down,
        )

    def start(self):
        for upward in (True, False):
            @pl.when(self.sends(upward, 1))
            def _():
                self.along(upward, 1).start()

    def pump(self, d):
        z = self.at.z
        for upward in (True, False):
            i = d - 1 if upward else 2 + d
            @pl.when(self.comes(upward, d))
            def _():
                part = self.ref.at[z - d if upward else z + d]
                rcopy(part, part, self.zs.at[i], self.zr.at[i], self.at.core).wait_recv()
                if d < 3:
                    @pl.when(self.sends(upward, d + 1))
                    def _():
                        self.along(upward, d + 1).start()

    def finish(self):
        for d in (1, 2, 3):
            for upward in (True, False):
                @pl.when(self.sends(upward, d))
                def _():
                    self.along(upward, d).wait_send()


class PlaneSum:
    def __init__(self, at, x_first, base, rows, acc, r1, r2, eb, ss, rs):
        self.acc, self.eb = acc, eb
        self.ss, self.rs = ss, rs
        self.base, self.h, self.w = base, rows // 2, rows // 4
        self.r1, self.r2 = r1.at[pl.ds(base // 2, self.h)], r2.at[pl.ds(base // 4, self.w)]
        if x_first:
            self.bf, self.bs, self.nf, self.ns = at.xb, at.yb, at.xn, at.yn
        else:
            self.bf, self.bs, self.nf, self.ns = at.yb, at.xb, at.yn, at.xn
        self.k1 = base + self.h * self.bf
        self.k2 = self.k1 + self.w * self.bs

    def back(self, rows):
        return self.eb.at[:, rows] if len(self.eb.shape) == 3 else self.eb.at[rows]

    def rows1(self):
        return pl.ds(self.k1, self.h)

    def rows2(self):
        return pl.ds(self.k2, self.w)

    def c1(self):
        other = pl.ds(self.base + self.h * (1 - self.bf), self.h)
        return rcopy(self.acc.at[other], self.r1, self.ss.at[0], self.rs.at[0], self.nf)

    def c2(self):
        other = pl.ds(self.k1 + self.w * (1 - self.bs), self.w)
        return rcopy(self.acc.at[other], self.r2, self.ss.at[1], self.rs.at[1], self.ns)

    def c3(self):
        part = self.back(self.rows2())
        return rcopy(part, part, self.ss.at[2], self.rs.at[2], self.ns)

    def c4(self):
        part = self.back(self.rows1())
        return rcopy(part, part, self.ss.at[3], self.rs.at[3], self.nf)

    def w3(self):
        part = self.back(pl.ds(self.k1 + self.w * (1 - self.bs), self.w))
        rcopy(part, part, self.ss.at[2], self.rs.at[2], self.ns).wait_recv()

    def w4(self):
        part = self.back(pl.ds(self.base + self.h * (1 - self.bf), self.h))
        rcopy(part, part, self.ss.at[3], self.rs.at[3], self.nf).wait_recv()

    def go1(self):
        self.c1().start()

    def go2(self):
        self.c1().wait_recv()
        self.acc[self.rows1()] = self.acc[self.rows1()] + self.r1[...]
        self.c2().start()

    def total(self):
        self.c2().wait_recv()
        return self.acc[self.rows2()] + self.r2[...]

    def go3(self, value):
        if len(self.eb.shape) == 3:
            high, low = split(value)
            self.eb[0, self.rows2()] = high
            self.eb[1, self.rows2()] = low
        else:
            self.eb[self.rows2()] = value.astype(BF)
        self.c3().start()

    def go4(self):
        self.w3()
        self.c4().start()

    def end(self):
        self.w4()

    def finish(self):
        for c in (self.c1(), self.c2(), self.c3(), self.c4()):
            c.wait_send()


class GlobalSum:
    def __init__(self, at, sums, zsums, ss, rs):
        self.at, self.sums, self.zsums, self.ss, self.rs = at, sums, zsums, ss, rs
        self.stages = [at.core, at.xn, at.yn]

    def near(self, j):
        return rcopy(self.sums.at[2 * j], self.sums.at[2 * j + 1], self.ss.at[j], self.rs.at[j], self.stages[j])

    def far(self, o, src):
        return rcopy(self.sums.at[6], self.zsums.at[src], self.ss.at[3 + o], self.rs.at[3 + o], self.at.peers[o])

    def start(self, value):
        self.sums[0] = jnp.full((8, 128), value, F32)
        self.near(0).start()

    def result(self):
        z, sums, zsums = self.at.z, self.sums, self.zsums
        for j in range(3):
            self.near(j).wait_recv()
            sums[2 * j + 2] = sums[2 * j] + sums[2 * j + 1]
            if j < 2:
                self.near(j + 1).start()
        zsums[z] = sums[6]
        for o in range(3):
            self.far(o, z).start()
        for o in range(3):
            self.far(o, lax.rem(z + 3 - o, 4)).wait_recv()
        return (zsums[0] + zsums[1]) + (zsums[2] + zsums[3])

    def finish(self):
        for j in range(3):
            self.near(j).wait_send()
        for o in range(3):
            self.far(o, self.at.z).wait_send()


def side_by_side(t, own, far):
    return jnp.where(t == 0, jnp.concatenate([own, far], 1), jnp.concatenate([far, own], 1))


def cuts(rows, i):
    large = rows // 2 + 32
    first = large if i % 2 == 0 else rows - large
    return [(0, first), (first, rows - first)]


def ns_kernel(
    p_ref, d_ref, out_ref, all_ref, xc, xa, hi, lo, delta, acc, r1, r2, eb, ox, sums, zsums,
    zs, zr, cs, cr, ps, pr, ms, mr, ds, dr, own_sem,
):
    at = Place()
    z, t = at.z, at.t
    half, n = p_ref.shape[0], p_ref.shape[1] // 2
    mine, others = pl.ds(t * half, half), pl.ds((1 - t) * half, half)
    at.greet()
    keep = pltpu.make_async_copy(d_ref, all_ref.at[z], own_sem)
    keep.start()
    moves = LineMoves(at, d_ref, all_ref, ds, dr)
    v = p_ref[...]
    xc[...] = v
    h, l = split(v)
    hi[z, mine] = h
    lo[z, mine] = l
    gathers = [
        [LineGather(at, ref, half, zs.at[g], zr.at[g], cs.at[g], cr.at[g]) for g, ref in pair]
        for pair in ([(0, hi), (1, lo)], [(2, delta.at[0])], [(3, delta.at[1])])
    ]
    for g in gathers[0]:
        g.start()
    norm = GlobalSum(at, sums, zsums, ms, mr)
    norm.start(jnp.sum(v * v))
    scale = None
    for step in range(3):
        sets = gathers[step]
        plane = [
            [
                PlaneSum(at, side == 0, base, size, acc.at[step, i], r1.at[step, i], r2.at[step, i],
                         eb.at[step, i], ps.at[step, i, side], pr.at[step, i, side])
                for side, (base, size) in enumerate(cuts(half, i))
            ]
            for i in range(4)
        ]

        def refresh(src):
            if step == 0:
                return
            old = hi[src].astype(F32) + lo[src].astype(F32)
            if step == 1:
                old = old * scale
            a, b = split(old + delta[step - 1, src].astype(F32))
            hi[src] = a
            lo[src] = b

        def partial(i):
            src = at.order[i]
            refresh(src)
            a, b = hi[z, mine], lo[z, mine]
            acc[step, i] = nt(a, hi[src]) + (nt(a, lo[src]) + nt(b, hi[src]))

        def centred(i):
            for p in plane[i]:
                total = p.total()
                if step == 0:
                    total = total * (scale * scale)
                row = lax.broadcasted_iota(jnp.int32, total.shape, 0)
                col = lax.broadcasted_iota(jnp.int32, total.shape, 1)
                shift = (z - at.order[i]) * (2 * half) + t * half + p.k2
                p.go3(jnp.where(row + shift == col, total - 1.0, total))

        def gather_in(i):
            for p in plane[i]:
                p.end()
            src = at.order[i]
            e = eb[step, i]
            term = nn(e, hi[src]) + nn(e, lo[src])
            if i == 0:
                xa[...] = term
            else:
                xa[...] += term

        for i in range(4):
            for g in sets:
                if i == 0:
                    g.own()
                else:
                    g.pump(i)
            if i > 1:
                for p in plane[i - 2]:
                    p.go4()
            if i > 0:
                for g in sets:
                    g.land(i)
                for p in plane[i - 1]:
                    p.go2()
            partial(i)
            for p in plane[i]:
                p.go1()
            if step == 0 and i == 0:
                whole = norm.result()
                scale = (0.9 * jnp.sqrt(D / (whole + 1e-06)))[0:1, 0:1]
            if i > 0:
                centred(i - 1)
            if i > 2:
                gather_in(i - 3)
        if step == 0:
            moves.start()
        else:
            moves.pump(step)
        for p in plane[2]:
            p.go4()
        gather_in(1)
        for p in plane[3]:
            p.go2()
        centred(3)
        gather_in(2)
        for p in plane[3]:
            p.go4()
        gather_in(3)
        for g in sets:
            g.finish()
        for pair in plane:
            for p in pair:
                p.finish()
        if step == 0:
            fresh = scale * (xc[...] - 0.5 * xa[...])
        else:
            fresh = xc[...] - 0.5 * xa[...]
        if step < 2:
            xc[...] = fresh
            held = hi[z, mine].astype(F32) + lo[z, mine].astype(F32)
            if step == 0:
                held = held * scale
            delta[step, z, mine] = (fresh - held).astype(BF)
            gathers[step + 1][0].start()
    left, right = fresh[:, :n], fresh[:, n:]
    ox[...] = jnp.where(t == 0, right, left)
    back = rcopy(ox, out_ref.at[mine], ms.at[7], mr.at[7], at.core)
    back.start()
    out_ref[mine] = jnp.where(t == 0, left, right)
    rcopy(ox, out_ref.at[others], ms.at[7], mr.at[7], at.core).wait_recv()
    back.wait_send()
    moves.pump(3)
    moves.finish()
    keep.wait()
    norm.finish()


def front_kernel(
    gt_ref, lt_ref, bt_ref, gain_ref, power_ref, stat_ref, rot_ref, clip_ref, gx, lx, bx, lpad, gall, hi, lo,
    bc, ra, oy, bs, br, g_ref, l_ref, b_ref,
    acc, r1, r2, eb, ox, sums, zsums, zs, zr, cs, cr, ps, pr, ms, mr, xs, xr,
):
    at = Place()
    z, t = at.z, at.t
    n = g_ref.shape[1]
    half = g_ref.shape[0] // 2
    mine, others = pl.ds(t * half, half), pl.ds((1 - t) * half, half)
    g_ref[...] = gt_ref[...].T
    at.greet()
    swaps = [
        rcopy(ref.at[others], dst, xs.at[i], xr.at[i], at.core)
        for i, (ref, dst) in enumerate([(g_ref, gx), (b_ref, bx), (l_ref, lx)])
    ]
    swaps[0].start()
    for one, ref, src in ((swaps[1], b_ref, bt_ref), (swaps[2], l_ref, lt_ref)):
        ref[...] = src[...].T
        one.start()
    grads = LineGather(at, gall, half, zs.at[0], zr.at[0], cs.at[0], cr.at[0])
    bases = [
        LineGather(at, ref, half, zs.at[1 + i], zr.at[1 + i], cs.at[1 + i], cr.at[1 + i])
        for i, ref in enumerate([hi, lo])
    ]
    swaps[0].wait_recv()
    gall[z, mine] = side_by_side(t, g_ref[mine], gx[...])
    grads.start()
    gf = g_ref[...].astype(F32)
    norm = GlobalSum(at, sums, zsums, ms, mr)
    norm.start(jnp.sum(gf * gf) + jnp.sum(gain_ref[...] * gain_ref[...]) * 0.125)
    swaps[1].wait_recv()
    h, l = split(side_by_side(t, b_ref[mine], bx[...]))
    hi[z, mine] = h
    lo[z, mine] = l
    swaps[2].wait_recv()
    own, far = l_ref[mine], lx[...]
    zero = jnp.zeros_like(own)
    for j in range(2):
        block = jnp.where(t == j, own, far)
        lpad[j] = side_by_side(at.xb, block, zero)
    whole = norm.result()
    clip = jnp.minimum(1.0, D / jnp.sqrt(whole + 1e-06))
    clip_ref[...] = clip
    coef = (0.05 / D * clip * clip)[0:1, 0:1]
    plane = [
        [
            PlaneSum(at, side == 0, base, size, acc.at[i], r1.at[i], r2.at[i],
                     eb.at[at.order[i]], ps.at[i, side], pr.at[i, side])
            for side, (base, size) in enumerate(cuts(half, i))
        ]
        for i in range(4)
    ]

    def partial(i):
        src = at.order[i]
        mix = jnp.where(src % 2 == at.yb, 0.95, 0.0).astype(F32)
        acc[i] = coef * nt(gall[z, mine], gall[src]) + mix * lpad[src // 2]

    def centred(i):
        for p in plane[i]:
            p.go3(p.total())

    near_x, near_y = at.xb == t, at.yb == z % 2
    origin = jnp.logical_and(near_x, near_y)
    relay = jnp.logical_and(near_x, jnp.logical_not(near_y))

    def spread(i, axis, j):
        part = bc.at[at.order[i], j]
        return rcopy(part, part, bs.at[axis, i, j], br.at[axis, i, j], at.yn if axis else at.xn)

    def spread_start(i):
        src = at.order[i]

        @pl.when(origin)
        def _():
            for j, ref in enumerate((hi, lo)):
                v = ref[src].astype(F32)
                bc[src, j] = jnp.where(z < 2, v[:, :n], v[:, n:]).astype(BF)
                spread(i, 1, j).start()
                spread(i, 0, j).start()

    def spread_relay(i):
        @pl.when(relay)
        def _():
            for j in range(2):
                spread(i, 1, j).wait_recv()
                spread(i, 0, j).start()

    def rotate(i):
        @pl.when(jnp.logical_not(near_x))
        def _():
            for j in range(2):
                spread(i, 0, j).wait_recv()

        src = at.order[i]
        term = tn(bc[src, 0], gall[src]) + tn(bc[src, 1], gall[src])
        if i == 0:
            ra[...] = term
        else:
            ra[...] += term

    for i in range(4):
        if i == 0:
            grads.own()
        else:
            grads.pump(i)
            if i == 1:
                for b in bases:
                    b.start()
            if i > 1:
                for p in plane[i - 2]:
                    p.go4()
            grads.land(i)
            for p in plane[i - 1]:
                p.go2()
        partial(i)
        for p in plane[i]:
            p.go1()
        if i > 0:
            centred(i - 1)
        if i == 1:
            for b in bases:
                b.own()
            spread_start(0)
        if i == 3:
            spread_relay(0)
    for p in plane[2]:
        p.go4()
    for b in bases:
        b.pump(1)
    for p in plane[3]:
        p.go2()
    centred(3)
    for b in bases:
        b.land(1)
    spread_start(1)
    for p in plane[3]:
        p.go4()
    rotate(0)
    for i in range(4):
        for p in plane[i]:
            p.end()
        if i > 1:
            for b in bases:
                b.pump(i)
            for b in bases:
                b.land(i)
            spread_start(i)
        src = at.order[i]
        sh, sl = eb[src, 0], eb[src, 1]
        term = nn(sh, hi[src]) + (nn(sh, lo[src]) + nn(sl, hi[src]))
        if i == 0:
            power_ref[...] = term
        else:
            power_ref[...] += term
        if i > 1:
            spread_relay(i - 1)
        if i > 2:
            rotate(i - 2)
    spread_relay(3)
    for j, place in ((0, t), (1, 1 - t)):
        c = 2 * place + at.yb
        v = eb[c, 0].astype(F32) + eb[c, 1].astype(F32)
        v = jnp.where(at.xb == 0, v[:, :n], v[:, n:])
        if j == 0:
            stat_ref[mine] = v
        else:
            ox[...] = v
    back = rcopy(ox, stat_ref.at[mine], xs.at[3], xr.at[3], at.core)
    back.start()
    rotate(2)
    rotate(3)
    turned = clip[0:1, 0:1] * ra[...]
    oy[...] = jnp.where(t == 0, turned[:, n:], turned[:, :n])
    rot_back = rcopy(oy, rot_ref.at[mine], xs.at[4], xr.at[4], at.core)
    rot_back.start()
    rot_ref[mine] = jnp.where(t == 0, turned[:, :n], turned[:, n:])
    rcopy(ox, stat_ref.at[others], xs.at[3], xr.at[3], at.core).wait_recv()
    rcopy(oy, rot_ref.at[others], xs.at[4], xr.at[4], at.core).wait_recv()
    back.wait_send()
    rot_back.wait_send()
    for i in range(4):
        @pl.when(near_x)
        def _():
            for j in range(2):
                spread(i, 0, j).wait_send()

        @pl.when(origin)
        def _():
            for j in range(2):
                spread(i, 1, j).wait_send()

    grads.finish()
    for b in bases:
        b.finish()
    for pair in plane:
        for p in pair:
            p.finish()
    norm.finish()
    for one in swaps:
        one.wait_send()


def front(gradient, statistic, basis, gain):
    rows, n = gradient.shape
    half = rows // 2
    dma = pltpu.SemaphoreType.DMA
    vmem = pl.BlockSpec(memory_space=pltpu.VMEM)
    return pl.pallas_call(
        front_kernel,
        out_shape=(
            jax.ShapeDtypeStruct((half, 2 * n), F32),
            jax.ShapeDtypeStruct((rows, n), F32),
            jax.ShapeDtypeStruct((rows, n), F32),
            jax.ShapeDtypeStruct((8, 128), F32),
        ),
        in_specs=[vmem] * 4,
        out_specs=(vmem,) * 4,
        cost_estimate=pl.CostEstimate(flops=10**11, bytes_accessed=4 * 10**8, transcendentals=0),
        scratch_shapes=[
            pltpu.VMEM((half, n), BF),
            pltpu.VMEM((half, n), F32),
            pltpu.VMEM((half, n), F32),
            pltpu.VMEM((2, half, 2 * n), F32),
            pltpu.VMEM((4, rows, 2 * n), BF),
            pltpu.VMEM((4, rows, 2 * n), BF),
            pltpu.VMEM((4, rows, 2 * n), BF),
            pltpu.VMEM((4, 2, rows, n), BF),
            pltpu.VMEM((half, 2 * n), F32),
            pltpu.VMEM((half, n), F32),
            dma((2, 4, 2)), dma((2, 4, 2)),
            pltpu.VMEM((rows, n), BF), pltpu.VMEM((rows, n), F32), pltpu.VMEM((rows, n), F32),
            pltpu.VMEM((4, half, rows), F32),
            pltpu.VMEM((4, half // 2, rows), F32),
            pltpu.VMEM((4, half // 4, rows), F32),
            pltpu.VMEM((4, 2, half, rows), BF),
            pltpu.VMEM((half, n), F32),
            pltpu.VMEM((7, 8, 128), F32),
            pltpu.VMEM((4, 8, 128), F32),
            dma((3, 6)), dma((3, 6)), dma((3, 7)), dma((3, 7)),
            dma((4, 2, 4)), dma((4, 2, 4)), dma((8,)), dma((8,)), dma((5,)), dma((5,)),
        ],
        compiler_params=pltpu.CompilerParams(
            collective_id=8, has_side_effects=True, vmem_limit_bytes=56 << 20
        ),
    )(gradient.T, statistic.T, basis.T, gain)


def newton_schulz(p, extra):
    half, rows = p.shape
    n = rows // 2
    rows = 2 * half
    dma = pltpu.SemaphoreType.DMA
    return pl.pallas_call(
        ns_kernel,
        out_shape=(
            jax.ShapeDtypeStruct((rows, n), F32),
            jax.ShapeDtypeStruct((4, *extra.shape), extra.dtype),
        ),
        in_specs=[pl.BlockSpec(memory_space=pltpu.VMEM), pl.BlockSpec(memory_space=pl.ANY)],
        out_specs=(pl.BlockSpec(memory_space=pltpu.VMEM), pl.BlockSpec(memory_space=pl.ANY)),
        cost_estimate=pl.CostEstimate(flops=10**11, bytes_accessed=10**9, transcendentals=0),
        scratch_shapes=[
            pltpu.VMEM((half, 2 * n), F32),
            pltpu.VMEM((half, 2 * n), F32),
            pltpu.VMEM((4, rows, 2 * n), BF),
            pltpu.VMEM((4, rows, 2 * n), BF),
            pltpu.VMEM((2, 4, rows, 2 * n), BF),
            pltpu.VMEM((3, 4, half, rows), F32),
            pltpu.VMEM((3, 4, half // 2, rows), F32),
            pltpu.VMEM((3, 4, half // 4, rows), F32),
            pltpu.VMEM((3, 4, half, rows), BF),
            pltpu.VMEM((half, n), F32),
            pltpu.VMEM((7, 8, 128), F32),
            pltpu.VMEM((4, 8, 128), F32),
            dma((4, 6)), dma((4, 6)), dma((4, 7)), dma((4, 7)),
            dma((3, 4, 2, 4)), dma((3, 4, 2, 4)), dma((8,)), dma((8,)),
            dma((6,)), dma((6,)), dma(()),
        ],
        compiler_params=pltpu.CompilerParams(
            collective_id=7, has_side_effects=True, vmem_limit_bytes=60 << 20
        ),
    )(p, extra)


def matmul(left_side, right_side):
    return jnp.dot(
        left_side, right_side, precision=lax.Precision.HIGH, preferred_element_type=jnp.float32
    )


def row_panel(local_block):
    return lax.all_gather(local_block, GROUP, axis=1, tiled=True)


def same(block):
    return block


def pack(block):
    top = jnp.max(jnp.abs(block), axis=0, keepdims=True)
    power = jnp.clip(jnp.ceil(jnp.log2(jnp.maximum(top, 1e-30))) - 14.0, -110.0, 120.0)
    scaled = block * jnp.exp2(-power)
    tail = jnp.broadcast_to(power, (PAD, block.shape[1]))
    return jnp.concatenate([scaled, tail], axis=0).astype(jnp.float16)


def unpack(payload):
    values = payload.astype(jnp.float32)
    return values[..., :-PAD, :] * jnp.exp2(values[..., -PAD : -PAD + 1, :])


def partners(size):
    if size & (size - 1) == 0:
        return [[(one, one ^ offset) for one in range(size)] for offset in range(1, size)]
    return [
        [(one, (one + offset) % size) for one in range(size)] for offset in range(1, size)
    ]


def place_of_source(place, offset, size):
    return place ^ offset if size & (size - 1) == 0 else (place - offset) % size


def place_of_target(place, offset, size):
    return place ^ offset if size & (size - 1) == 0 else (place + offset) % size


def shard_total(value, shards):
    if shards > 8:
        return lax.psum(value, "shard")
    tile = jnp.full((8, 128), value, jnp.float32)
    total = value
    for pairs in partners(shards):
        total = total + lax.ppermute(tile, "shard", pairs)[0, 0]
    return total


def rows_times_shards(full_rows, block, shards, place, encode, decode):
    if shards > 8:
        gathered = decode(lax.all_gather(encode(block), "shard", axis=0))
        return matmul(full_rows, gathered.reshape(-1, block.shape[1]))
    rows = block.shape[0]
    sent = encode(block)
    pieces = [block] + [
        decode(lax.ppermute(sent, "shard", pairs)) for pairs in partners(shards)
    ]
    total = None
    for offset, piece in enumerate(pieces):
        source = place_of_source(place, offset, shards)
        left = lax.dynamic_slice_in_dim(full_rows, source * rows, rows, 1)
        term = matmul(left, piece)
        total = term if total is None else total + term
    return total


def scatter_product(full_rows, block, shards, place, encode, decode):
    if shards > 8:
        return lax.psum_scatter(
            matmul(full_rows.T, block), "shard", scatter_dimension=0, tiled=True
        )
    rows = full_rows.shape[1] // shards
    arrived = []
    for offset, pairs in enumerate(partners(shards), 1):
        target = place_of_target(place, offset, shards)
        chunk = matmul(lax.dynamic_slice_in_dim(full_rows, target * rows, rows, 1).T, block)
        arrived.append(lax.ppermute(encode(chunk), "shard", pairs))
    total = matmul(lax.dynamic_slice_in_dim(full_rows, place * rows, rows, 1).T, block)
    for payload in arrived:
        total = total + decode(payload)
    return total


def outer_block(gradient, grad_rows, shards, group, place, member):
    rows, cols = gradient.shape
    if rows % cols == 0 and shards <= 8:
        own = lax.dynamic_slice_in_dim(grad_rows, (member * cols) % rows, cols, 0)
        other = jnp.zeros_like(own)
        for offset in range(1, shards):
            pairs = []
            for column in range(group):
                home = column * cols // rows
                pairs.append(
                    (home * group + column, (home + offset) % shards * group + column)
                )
            other = other + lax.ppermute(own, EVERY, pairs)
        partner = jnp.where(place == member * cols // rows, own, other)
        return jnp.dot(grad_rows, partner.T, preferred_element_type=jnp.float32)
    partner = lax.all_gather(gradient, "shard", axis=0, tiled=True)
    product = jnp.dot(gradient, partner.T, preferred_element_type=jnp.float32)
    return lax.psum_scatter(product, GROUP, scatter_dimension=1, tiled=True)


def plain(
    gradient,
    gain_grad,
    left_statistic,
    left_basis,
    first_moment,
    second_moment,
    norm_gains,
    gain_first,
    gain_second,
):
    group = lax.axis_size(GROUP)
    shards = lax.axis_size("shard")
    place = lax.axis_index("shard")
    member = lax.axis_index(GROUP)
    rows, cols = gradient.shape
    grad_float = gradient.astype(jnp.float32)
    grad_rows = row_panel(gradient)
    late_basis, grad_rows = lax.optimization_barrier((left_basis, grad_rows))
    basis_rows = row_panel(late_basis)
    grad_rows_float = grad_rows.astype(jnp.float32)
    squares_total = shard_total(
        jnp.sum(grad_rows_float * grad_rows_float) + jnp.sum(gain_grad * gain_grad), shards
    )
    clip_factor = jnp.minimum(1.0, D / jnp.sqrt(squares_total + 1e-06))
    outer_part = outer_block(gradient, grad_rows, shards, group, place, member)
    new_statistic = 0.95 * left_statistic + (0.05 / D * clip_factor * clip_factor) * outer_part
    ready_statistic, basis_rows = lax.optimization_barrier((new_statistic, basis_rows))
    statistic_rows = row_panel(ready_statistic)
    power_product = rows_times_shards(
        statistic_rows, left_basis, shards, place, same, same
    )
    power_rows = row_panel(power_product)
    rotated = clip_factor * scatter_product(
        basis_rows, grad_float, shards, place, same, same
    )
    new_first = 0.9 * first_moment + 0.1 * rotated
    new_second = 0.95 * second_moment + 0.05 * rotated * rotated
    direction = new_first / (jnp.sqrt(new_second) + 1e-08)
    update = rows_times_shards(
        basis_rows,
        direction,
        shards,
        place,
        lambda x: x.astype(jnp.float16),
        lambda x: x.astype(jnp.float32),
    )
    update, power_rows = lax.optimization_barrier((update, power_rows))
    power_sum = shard_total(jnp.sum(power_rows * power_rows), shards)
    scale = 0.9 * jnp.sqrt(D / (power_sum + 1e-06))
    iterate = scale * power_product
    iterate_rows = scale * power_rows
    row_index = place * rows + lax.broadcasted_iota(jnp.int32, (rows, cols), 0)
    col_index = member * cols + lax.broadcasted_iota(jnp.int32, (rows, cols), 1)
    eye = (row_index == col_index).astype(jnp.float32)
    for sweep_index in range(NS_STEPS):
        if sweep_index:
            iterate_rows = row_panel(iterate)
            gram_block = scatter_product(
                iterate_rows, iterate, shards, place, pack, unpack
            )
        else:
            gram_block = (scale * scale) * scatter_product(
                power_rows, power_product, shards, place, pack, unpack
            )
        iterate = iterate - 0.5 * rows_times_shards(
            iterate_rows, gram_block - eye, shards, place, pack, unpack
        )
    gain_clipped = clip_factor * gain_grad
    new_gain_first = 0.9 * gain_first + 0.1 * gain_clipped
    new_gain_second = 0.95 * gain_second + 0.05 * gain_clipped * gain_clipped
    new_gains = norm_gains - 0.01 * new_gain_first / (jnp.sqrt(new_gain_second) + 1e-08)
    return (
        update,
        new_first,
        new_second,
        new_statistic,
        iterate,
        new_gains,
        new_gain_first,
        new_gain_second,
    )


def parts(v):
    high = lax.reduce_precision(v, 8, 7)
    return high.astype(BF), (v - high).astype(BF)


def fast(
    gradient,
    gain_grad,
    left_statistic,
    left_basis,
    first_moment,
    second_moment,
    norm_gains,
    gain_first,
    gain_second,
):
    power, new_statistic, rotated, clip_tile = front(
        gradient, left_statistic, left_basis, gain_grad
    )
    clip_factor = clip_tile[0, 0]
    power, rotated, late_basis = lax.optimization_barrier((power, rotated, left_basis))
    basis_high, basis_low = parts(late_basis)
    rows = late_basis.shape[0]
    basis_rows = row_panel(jnp.concatenate([basis_high, basis_low], 0))
    new_first = 0.9 * first_moment + 0.1 * rotated
    new_second = 0.95 * second_moment + 0.05 * rotated * rotated
    direction = new_first / (jnp.sqrt(new_second) + 1e-08)
    new_basis, all_rows = newton_schulz(power, jnp.stack(parts(direction)))
    high = all_rows[:, 0].reshape(-1, direction.shape[1])
    low = all_rows[:, 1].reshape(-1, direction.shape[1])
    terms = nn(basis_rows, high)
    update = terms[:rows] + (terms[rows:] + nn(basis_rows[:rows], low))
    gain_clipped = clip_factor * gain_grad
    new_gain_first = 0.9 * gain_first + 0.1 * gain_clipped
    new_gain_second = 0.95 * gain_second + 0.05 * gain_clipped * gain_clipped
    new_gains = norm_gains - 0.01 * new_gain_first / (jnp.sqrt(new_gain_second) + 1e-08)
    return (
        update,
        new_first,
        new_second,
        new_statistic,
        new_basis,
        new_gains,
        new_gain_first,
        new_gain_second,
    )


def solution(mesh):
    sizes = tuple(mesh.shape[name] for name in EVERY)
    on_device = fast if sizes == (4, 2, 4) else plain
    matrix = P("shard", GROUP)
    vector = P(None, "shard")
    return jax.shard_map(
        on_device,
        mesh=mesh,
        in_specs=(
            matrix,
            vector,
            matrix,
            matrix,
            matrix,
            matrix,
            vector,
            vector,
            vector,
        ),
        out_specs=(matrix, matrix, matrix, matrix, matrix, vector, vector, vector),
        check_vma=False,
    )
```
